256 devices in a mesh: gx: 8 (over z), gy: 16 (over y, x), sa: 2 (over core).
Axes of the slice: x: 4, y: 4, z: 8, core: 2. Of those that a mesh axis runs over, the one named last changes fastest.
Arguments:
- field: float32 [33, 32, 672, 256], P(None, 'gx', 'gy', 'sa'), as said below
- start: float32 [33, 16], replicated, may hold values from -1 to 1
Outputs:
- basis: float32 [33, 16], replicated
- gram_two: float32 [672, 672], P('gy', ('gx', 'sa'))
The draws below stay inside these ranges and needn't reach their ends.
Inputs may be any that keep to these rules, and one draw needn't show every extreme that they name: `field`: every entry is finite; species differ in scale.
All inputs are finite; a program needn't handle non-finite values.
Results may differ from the reference program's by a relative error of at most 0.0003.
Values sent between devices are 32-bit elements; how exact they have to be, the bound alone decides.
A program may use at most 128 MiB of HBM per device.

```python
import jax
import jax.numpy as jnp
from jax import lax

S = 33
R = 16
ITERS = 4
NX = 32
NY = 672
NZ = 256


def draw_field(key, part):
    keys = jax.random.split(key, 5)
    shape = (S, NX, NY, NZ)
    mode_count = 48
    species_scale = jnp.exp(jax.random.uniform(keys[0], (S, 1, 1, 1), jnp.float32) * jnp.log(10.0))
    position = jnp.arange(NX, dtype=jnp.float32).reshape(1, NX, 1, 1)
    rising = jnp.sqrt(1.0 + 2.0 * position / max(NX - 1, 1))
    weight_y = jax.random.uniform(keys[1], (1, 1, NY, 1), jnp.float32, 0.5, 1.5)
    profiles = jax.random.normal(keys[4], (mode_count, NY), jnp.float32)
    noise = jax.random.normal(keys[2], shape, jnp.float32)
    mode_loads = jax.random.normal(keys[3], (S, NX, mode_count, NZ), jnp.float32)
    common = jnp.einsum('sxmz,my->sxyz', mode_loads, profiles, precision=lax.Precision.HIGHEST) / jnp.sqrt(float(mode_count))
    return species_scale * rising * (noise + common * weight_y)


def scatter_about(own_key, extent, deviation, reach, kind=jnp.bfloat16):
    drawn = jax.random.normal(own_key, extent, jnp.float32) * deviation
    return jnp.minimum(jnp.maximum(drawn, -reach), reach).astype(kind)


def setup_inputs(seed: int = 0) -> dict:
    seeds = jax.random.split(jax.random.key(seed), 3)
    field = draw_field(jax.random.fold_in(seeds[2], 71), 0)
    start = scatter_about(seeds[1], (S, R), S ** -0.5, 1.0, jnp.float32)
    return {"field": field, "start": start}


HIGH = lax.Precision.HIGHEST

def orth(block):
    inner = jnp.dot(block.T.astype(jnp.float32), block.astype(jnp.float32), precision=HIGH, preferred_element_type=jnp.float32)
    lower = jnp.linalg.cholesky(inner)
    return jax.scipy.linalg.solve_triangular(lower, block.T, lower=True).T

def leading(gram, start):
    basis = orth(orth(start))
    for step in range(ITERS):
        basis = orth(orth(jnp.dot(gram.astype(jnp.float32), basis.astype(jnp.float32), precision=HIGH, preferred_element_type=jnp.float32)))
    return basis

def reference(field, start):
    flat = field.reshape(S, -1)
    species_gram = jnp.dot(flat.astype(jnp.float32), flat.T.astype(jnp.float32), precision=HIGH, preferred_element_type=jnp.float32) / (NX * NY * NZ)
    basis = leading(species_gram, start)
    core = jnp.einsum('sr,sxyz->rxyz', basis, field, precision=HIGH)
    gram_two = jnp.einsum('rxiz,rxjz->ij', core, core, precision=HIGH) / (R * NX * NZ)
    return (basis, gram_two)
```

```python
import functools
import math

import jax
import jax.numpy as jnp
from jax import lax
from jax.experimental import pallas as pl
from jax.experimental.pallas import tpu as pltpu
from jax.sharding import PartitionSpec as P

ITERS = 4
F32 = jnp.float32
BF16 = jnp.bfloat16
HIGH = lax.Precision.HIGHEST
LANES = 128
SP = 48
YP = 48
NT = (((1,), (1,)), ((), ()))


def split(value):
    high = value.astype(BF16)
    return high, (value - high.astype(F32)).astype(BF16)


def orth(w, ranks):
    products = (w[:, None, :] * w[None, :, :]).reshape(ranks * ranks, LANES)
    first, rest = split(products)
    second, third = split(products - first.astype(F32))
    ones = jnp.ones((LANES, LANES), BF16)
    inner = (
        jnp.dot(first, ones, preferred_element_type=F32)
        + jnp.dot(second, ones, preferred_element_type=F32)
        + jnp.dot(third, ones, preferred_element_type=F32)
    )
    lines = [inner[i * ranks : (i + 1) * ranks] for i in range(ranks)]
    row = lax.broadcasted_iota(jnp.int32, (ranks, LANES), 0)
    pivots = jnp.ones((ranks, LANES), F32)
    for j in range(ranks):
        line = lines[j]
        pivots = jnp.where(row == j, line, pivots)
        factor = line * (1.0 / line[j : j + 1])
        if j + 1 < ranks:
            below = jnp.where(row > j, factor, 0.0)
            w = w - below * w[j : j + 1]
            for i in range(j + 1, ranks):
                lines[i] = lines[i] - factor[i : i + 1] * line
    return w * lax.rsqrt(pivots)


def kernel(cfg, field, start, basis_out, block_out, fv, hl, ub, zb, b_sa, b_x, b_y, b_z,
           core, mid0, mid1, recv, ah, al, gs, go, gr, r1a, r1b, t0, t1, r2a, r2b, hb, pack, r3,
           load_sem, ssem, rsem):
    nx, ny, nz, ns = cfg["nx"], cfg["ny"], cfg["nz"], 2
    species, cx, cy, cz = field.shape
    ranks = start.shape[1]
    gx, gy, sa = lax.axis_index("gx"), lax.axis_index("gy"), lax.axis_index("sa")
    mx, my = lax.rem(gy, nx), gy // nx

    def to_sa(d):
        return {"sa": 1 - sa}

    def to_x(d):
        return {"gy": my * nx + lax.rem(mx + d, nx)}

    def to_y(d):
        return {"gy": lax.rem(my + d, ny) * nx + mx}

    def to_z(d):
        return {"gx": lax.rem(gx + d, nz)}

    used = [0]

    def send(src, dst, target):
        k = used[0]
        used[0] += 1
        copy = pltpu.make_async_remote_copy(
            src_ref=src, dst_ref=dst, send_sem=ssem.at[k], recv_sem=rsem.at[k],
            device_id=target, device_id_type=pl.DeviceIdType.MESH,
        )
        copy.start()
        return copy

    load = pltpu.make_async_copy(field, fv.at[0:species, :, 0:cy, :], load_sem)
    load.start()
    barrier = pltpu.get_barrier_semaphore()
    peers = [to_sa(1)] + [to_x(d) for d in range(1, nx)] + [to_y(d) for d in range(1, ny)]
    peers += [to_z(d) for d in range(1, nz)]
    for peer in peers:
        pl.semaphore_signal(barrier, inc=1, device_id=peer, device_id_type=pl.DeviceIdType.MESH)
    fv[species:SP] = jnp.zeros((SP - species, cx, YP, cz), F32)
    ub[...] = jnp.zeros(ub.shape, F32)
    zb[...] = jnp.zeros(zb.shape, F32)
    zb[0:species, 0:ranks] = start[...]
    load.wait()

    flat = fv.reshape(SP * cx * YP, cz)
    step = cfg["step"]
    wide = step * cz
    total = jnp.zeros((2 * SP, SP), F32)
    for x in range(cx):
        for g in range(cy // step):
            cols = [flat[pl.ds(x * YP + g * step + k, SP, stride=cx * YP), :] for k in range(step)]
            high, low = split(jnp.concatenate(cols, axis=1))
            both = jnp.concatenate([high, low], axis=0)
            at = (x * (cy // step) + g) * wide
            hl[:, at : at + wide] = both
            total = total + lax.dot_general(both, high, NT, preferred_element_type=F32)
    ub[0:SP, 0:SP] = total[0:SP] * 0.5 + total[SP:]
    lane = lax.broadcasted_iota(jnp.int32, (SP, LANES), 1)
    half = ub[...]
    packed = half[0:16] + pltpu.roll(half[16:32], 42, 1) + pltpu.roll(half[32:48], 84, 1)

    pl.semaphore_wait(barrier, len(peers))

    def start_sum(value, buf, n, me, target):
        buf[me] = value
        return [send(buf.at[me], buf.at[me], target(d)) for d in range(1, n)]

    def end_sum(copies, buf, n):
        for copy in copies:
            copy.wait()
        out = buf[0]
        for k in range(1, n):
            out = out + buf[k]
        return out

    packed = end_sum(start_sum(packed, b_sa, ns, sa, to_sa), b_sa, ns)
    packed = end_sum(start_sum(packed, b_x, nx, mx, to_x), b_x, nx)
    packed = end_sum(start_sum(packed, b_y, ny, my, to_y), b_y, ny)
    copies = start_sum(packed, b_z, nz, gx, to_z)
    w = zb[...].T[0:ranks]
    w = orth(orth(w, ranks), ranks)
    packed = end_sum(copies, b_z, nz)

    scale = 1.0 / cfg["cells"]
    packed = packed * scale
    ub[0:16] = packed
    ub[16:32] = pltpu.roll(packed, LANES - 42, 1)
    ub[32:48] = pltpu.roll(packed, LANES - 84, 1)
    srow = lax.broadcasted_iota(jnp.int32, (SP, LANES), 0)
    half = jnp.where((lane < species) & (srow < species), ub[...], 0.0)
    zb[...] = jnp.zeros(zb.shape, F32)
    zb[0:SP] = half
    half = zb[...]
    gram = half + half.T

    def round_(i, w):
        w = jnp.dot(w, gram, precision=HIGH, preferred_element_type=F32)
        return orth(orth(w, ranks), ranks)

    w = lax.fori_loop(0, ITERS, round_, w)

    whigh = w.astype(BF16).astype(F32)
    lhs = jnp.concatenate([whigh + pltpu.roll(whigh, SP, 1), w - whigh], axis=0).astype(BF16)
    lhs = lhs[:, 0 : 2 * SP]
    cflat = core.reshape(ranks * cx * YP, cz)

    def project(x):
        for g in range(cy // step):
            at = (x * (cy // step) + g) * wide
            out = jnp.dot(lhs, hl[:, at : at + wide], preferred_element_type=F32)
            out = out[0:ranks] + out[ranks:]
            for k in range(step):
                cflat[pl.ds(x * YP + g * step + k, ranks, stride=cx * YP), :] = (
                    out[:, k * cz : (k + 1) * cz]
                )

    hx = cx // 2
    for x in range(hx):
        project(x)
    first0 = []
    for d in range(1, nx):
        there = lax.rem(mx + d, nx)
        first0.append(send(core.at[:, there, 0:hx, 0:cy, :], mid0.at[:, :, mx, 0:cy, :], to_x(d)))
    for x in range(hx, cx):
        project(x)
    first1 = []
    for d in range(1, ny):
        there = lax.rem(my + d, ny)
        first1.append(send(core.at[there, :, hx:cx, 0:cy, :], mid1.at[:, :, my, 0:cy, :], to_y(d)))
    mid0[:, :, mx] = core[:, mx, 0:hx]
    mid1[:, :, my] = core[my, :, hx:cx]
    zb[0:ranks] = w
    basis_out[...] = zb[...].T[0:species, 0:ranks]
    for copy in first0:
        copy.wait()
    second = []
    for d in range(1, ny):
        there = lax.rem(my + d, ny)
        second.append(send(mid0.at[there, :, :, 0:cy, :], recv.at[0:hx, my, :, 0:cy, :], to_y(d)))
    recv[0:hx, my] = mid0[my]
    for copy in first1:
        copy.wait()
    for d in range(1, nx):
        there = lax.rem(mx + d, nx)
        second.append(send(mid1.at[there, :, :, 0:cy, :], recv.at[hx:cx, :, mx, 0:cy, :], to_x(d)))
    recv[hx:cx, :, mx] = mid1[mx]
    for copy in second:
        copy.wait()

    rows = ny * nx * YP
    for x in range(cx):
        high, low = split(recv[x].reshape(rows, cz))
        ah[:, :, :, x * cz : (x + 1) * cz] = high.reshape(nz, ns, YP, cz)
        al[:, :, :, x * cz : (x + 1) * cz] = low.reshape(nz, ns, YP, cz)
    depth = cx * cz
    columns = nz * YP
    lrows = ah.reshape(ny, nx * YP, depth), al.reshape(ny, nx * YP, depth)

    def gram_rows(y, side):
        lh, ll = lrows[0][y], lrows[1][y]
        rh, rl = ah[:, side].reshape(columns, depth), al[:, side].reshape(columns, depth)
        out = (
            lax.dot_general(lh, rh, NT, preferred_element_type=F32)
            + lax.dot_general(lh, rl, NT, preferred_element_type=F32)
            + lax.dot_general(ll, rh, NT, preferred_element_type=F32)
        )
        return out.reshape(nx, YP, columns)

    swaps = []
    for y in range(ny):
        gs[y] = gram_rows(y, 1 - sa)
        swaps.append(send(gs.at[y], gr.at[y], to_sa(1)))
    for y in range(ny):
        mine = gram_rows(y, sa)
        swaps[y].wait()
        go[y] = mine + gr[y]

    hy = YP // 2
    first0 = []
    for d in range(1, nx):
        there = lax.rem(mx + d, nx)
        first0.append(send(go.at[:, there, 0:hy, :], r1a.at[d - 1], to_x(d)))
    first1 = []
    for d in range(1, ny):
        there = lax.rem(my + d, ny)
        first1.append(send(go.at[there, :, hy:YP, :], r1b.at[d - 1], to_y(d)))
    for copy in first0:
        copy.wait()
    out = go[:, mx, 0:hy, :]
    for d in range(1, nx):
        out = out + r1a[d - 1]
    t0[...] = out
    second0 = []
    for d in range(1, ny):
        second0.append(send(t0.at[lax.rem(my + d, ny)], r2a.at[d - 1], to_y(d)))
    for copy in first1:
        copy.wait()
    out = go[my, :, hy:YP, :]
    for d in range(1, ny):
        out = out + r1b[d - 1]
    t1[...] = out
    second1 = []
    for d in range(1, nx):
        second1.append(send(t1.at[lax.rem(mx + d, nx)], r2b.at[d - 1], to_x(d)))
    for copy in second0:
        copy.wait()
    out = t0[my]
    for d in range(1, ny):
        out = out + r2a[d - 1]
    hb[0:hy, 0 : nz * YP] = out
    for copy in second1:
        copy.wait()
    out = t1[mx]
    for d in range(1, nx):
        out = out + r2b[d - 1]
    hb[hy:YP, 0 : nz * YP] = out

    fold = lax.broadcasted_iota(jnp.int32, (hy, LANES), 1) < LANES // 2
    for g in range(nz):
        tile = (g * YP) // LANES
        at = g * YP - tile * LANES
        parts = []
        for part in (hb[0:hy], hb[hy:YP]):
            piece = part[:, tile * LANES : (tile + 1) * LANES]
            if at:
                piece = pltpu.roll(piece, LANES - at, 1)
            if at + YP > LANES:
                other = part[:, (tile + 1) * LANES : (tile + 2) * LANES]
                where = lax.broadcasted_iota(jnp.int32, (hy, LANES), 1) < LANES - at
                piece = jnp.where(where, piece, pltpu.roll(other, LANES - at, 1))
            parts.append(piece)
        pack[g] = jnp.where(fold, parts[0], pltpu.roll(parts[1], LANES // 2, 1))
    last = []
    for d in range(1, nz):
        last.append(send(pack.at[lax.rem(gx + d, nz)], r3.at[d - 1], to_z(d)))
    out = pack[gx]
    for copy in last:
        copy.wait()
    for d in range(1, nz):
        out = out + r3[d - 1]
    out = out * (1.0 / cfg["terms"])
    block_out[0:hy, :] = out[:, 0:cy]
    block_out[hy:cy, :] = pltpu.roll(out, LANES // 2, 1)[0 : cy - hy, 0:cy]


def on_device(cfg, field, start):
    species, cx, cy, cz = field.shape
    ranks = start.shape[1]
    nx, ny, nz = cfg["nx"], cfg["ny"], cfg["nz"]
    cols = nz * YP
    colsp = -(-cols // LANES) * LANES
    hy = YP // 2
    hx = cx // 2
    cells = cx * cy * cz
    copies = 1 + (nx - 1) + (ny - 1) + (nz - 1) + 2 * (nx + ny - 2) + ny + 2 * (nx + ny - 2) + nz - 1
    vmem = pltpu.VMEM
    scratch = [
        vmem((SP, cx, YP, cz), F32), vmem((2 * SP, cells), BF16), vmem((SP, LANES), F32),
        vmem((LANES, LANES), F32), vmem((2, 16, LANES), F32), vmem((nx, 16, LANES), F32),
        vmem((ny, 16, LANES), F32), vmem((nz, 16, LANES), F32),
        vmem((ny, nx, cx, YP, cz), F32), vmem((ny, hx, nx, YP, cz), F32),
        vmem((nx, hx, ny, YP, cz), F32), vmem((cx, ny, nx, YP, cz), F32),
        vmem((nz, 2, YP, cx * cz), BF16), vmem((nz, 2, YP, cx * cz), BF16),
        vmem((ny, nx, YP, cols), F32), vmem((ny, nx, YP, cols), F32), vmem((ny, nx, YP, cols), F32),
        vmem((nx - 1, ny, hy, cols), F32), vmem((ny - 1, nx, hy, cols), F32),
        vmem((ny, hy, cols), F32), vmem((nx, hy, cols), F32),
        vmem((ny - 1, hy, cols), F32), vmem((nx - 1, hy, cols), F32),
        vmem((YP, colsp), F32), vmem((nz, hy, LANES), F32), vmem((nz - 1, hy, LANES), F32),
        pltpu.SemaphoreType.DMA, pltpu.SemaphoreType.DMA((copies,)), pltpu.SemaphoreType.DMA((copies,)),
    ]
    return pl.pallas_call(
        functools.partial(kernel, cfg),
        out_shape=(
            jax.ShapeDtypeStruct((species, ranks), F32),
            jax.ShapeDtypeStruct((cy, cy), F32),
        ),
        in_specs=[pl.BlockSpec(memory_space=pl.ANY), pl.BlockSpec(memory_space=vmem)],
        out_specs=(pl.BlockSpec(memory_space=vmem), pl.BlockSpec(memory_space=vmem)),
        scratch_shapes=scratch,
        compiler_params=pltpu.CompilerParams(
            collective_id=0, has_side_effects=True, vmem_limit_bytes=56 * 1024 * 1024
        ),
        name="tucker_step",
    )(field, start)


def solution(mesh):
    nz, n_plane, ns = mesh.shape["gx"], mesh.shape["gy"], mesh.shape["sa"]
    nx = math.isqrt(n_plane)
    cfg = dict(nx=nx, ny=n_plane // nx, nz=nz)

    def run(field, start):
        species, cx, cy, cz = field.shape
        ranks = start.shape[1]
        total = cx * nz * cz * ns
        full = dict(cfg, step=14 if cy % 14 == 0 else cy, cells=total * cy * n_plane, terms=ranks * total)
        return on_device(full, field, start)

    return jax.shard_map(
        run, mesh=mesh, in_specs=(P(None, "gx", "gy", "sa"), P()),
        out_specs=(P(), P("gy", ("gx", "sa"))), check_vma=False,
    )
```

```python
import functools
import math

import jax
import jax.numpy as jnp
from jax import lax
from jax.experimental import pallas as pl
from jax.experimental.pallas import tpu as pltpu
from jax.sharding import PartitionSpec as P

ITERS = 4
F32 = jnp.float32
BF16 = jnp.bfloat16
HIGH = lax.Precision.HIGHEST
LANES = 128
SP = 48
YP = 48
NT = (((1,), (1,)), ((), ()))


def split(value):
    high = value.astype(BF16)
    return high, (value - high.astype(F32)).astype(BF16)


def orth(w, ranks):
    products = (w[:, None, :] * w[None, :, :]).reshape(ranks * ranks, LANES)
    first, rest = split(products)
    second, third = split(products - first.astype(F32))
    ones = jnp.ones((LANES, LANES), BF16)
    inner = (
        jnp.dot(first, ones, preferred_element_type=F32)
        + jnp.dot(second, ones, preferred_element_type=F32)
        + jnp.dot(third, ones, preferred_element_type=F32)
    )
    lines = [inner[i * ranks : (i + 1) * ranks] for i in range(ranks)]
    row = lax.broadcasted_iota(jnp.int32, (ranks, LANES), 0)
    pivots = jnp.ones((ranks, LANES), F32)
    for j in range(ranks):
        line = lines[j]
        pivots = jnp.where(row == j, line, pivots)
        factor = line * (1.0 / line[j : j + 1])
        if j + 1 < ranks:
            below = jnp.where(row > j, factor, 0.0)
            w = w - below * w[j : j + 1]
            for i in range(j + 1, ranks):
                lines[i] = lines[i] - factor[i : i + 1] * line
    return w * lax.rsqrt(pivots)


def kernel(cfg, field, start, both_out, fv, hl, ub, zb, wb, b_sa, b_p, b_z,
           core, mid0, mid1, recv, ah, al, gs, go, gr, r1a, r1b, t0, t1, r2a, r2b, hb, pack, r3,
           load_sem, ssem, rsem):
    nx, ny, nz, ns = cfg["nx"], cfg["ny"], cfg["nz"], 2
    species, cz = field.shape[0], field.shape[2]
    cx, cy = cfg["cx"], cfg["cy"]
    ranks = start.shape[0]
    gx, gy, sa = lax.axis_index("gx"), lax.axis_index("gy"), lax.axis_index("sa")
    mx, my = lax.rem(gy, nx), gy // nx

    def to_sa(d):
        return {"sa": 1 - sa}

    def to_x(d):
        return {"gy": my * nx + lax.rem(mx + d, nx)}

    def to_y(d):
        return {"gy": lax.rem(my + d, ny) * nx + mx}

    def to_plane(d):
        return {"gy": lax.rem(my + d // nx, ny) * nx + lax.rem(mx + d % nx, nx)}

    def to_z(d):
        return {"gx": lax.rem(gx + d, nz)}

    used = [0]

    def send(src, dst, target):
        k = used[0]
        used[0] += 1
        copy = pltpu.make_async_remote_copy(
            src_ref=src, dst_ref=dst, send_sem=ssem.at[k], recv_sem=rsem.at[k],
            device_id=target, device_id_type=pl.DeviceIdType.MESH,
        )
        copy.start()
        return copy

    load = pltpu.make_async_copy(field, fv.at[0:species], load_sem)
    load.start()
    barrier = pltpu.get_barrier_semaphore()
    peers = [to_sa(1)] + [to_plane(d) for d in range(1, nx * ny)]
    peers += [to_z(d) for d in range(1, nz)]
    for peer in peers:
        pl.semaphore_signal(barrier, inc=1, device_id=peer, device_id_type=pl.DeviceIdType.MESH)
    fv[species:SP] = jnp.zeros((SP - species, cx * cy, cz), F32)
    ub[...] = jnp.zeros(ub.shape, F32)
    wb[...] = jnp.zeros(wb.shape, F32)
    wb[:, 0:species] = start[...]
    load.wait()

    flat = fv.reshape(SP * cx * cy, cz)
    step = cfg["step"]
    wide = step * cz
    total = jnp.zeros((2 * SP, SP), F32)
    for x in range(cx):
        for g in range(cy // step):
            cols = [flat[pl.ds((g * step + k) * cx + x, SP, stride=cx * cy), :] for k in range(step)]
            high, low = split(jnp.concatenate(cols, axis=1))
            both = jnp.concatenate([high, low], axis=0)
            at = (x * (cy // step) + g) * wide
            hl[:, at : at + wide] = both
            total = total + lax.dot_general(both, high, NT, preferred_element_type=F32)
    ub[0:SP, 0:SP] = total[0:SP] * 0.5 + total[SP:]
    lane = lax.broadcasted_iota(jnp.int32, (SP, LANES), 1)
    half = ub[...]
    packed = half[0:16] + pltpu.roll(half[16:32], 42, 1) + pltpu.roll(half[32:48], 84, 1)

    pl.semaphore_wait(barrier, len(peers))

    def start_sum(value, buf, n, me, target):
        buf[me] = value
        return [send(buf.at[me], buf.at[me], target(d)) for d in range(1, n)]

    def end_sum(copies, buf, n):
        for copy in copies:
            copy.wait()
        out = buf[0]
        for k in range(1, n):
            out = out + buf[k]
        return out

    packed = end_sum(start_sum(packed, b_sa, ns, sa, to_sa), b_sa, ns)
    packed = end_sum(start_sum(packed, b_p, nx * ny, gy, to_plane), b_p, nx * ny)
    copies = start_sum(packed, b_z, nz, gx, to_z)
    w = wb[...]
    w = orth(orth(w, ranks), ranks)
    packed = end_sum(copies, b_z, nz)

    scale = 1.0 / cfg["cells"]
    packed = packed * scale
    ub[0:16] = packed
    ub[16:32] = pltpu.roll(packed, LANES - 42, 1)
    ub[32:48] = pltpu.roll(packed, LANES - 84, 1)
    srow = lax.broadcasted_iota(jnp.int32, (SP, LANES), 0)
    half = jnp.where((lane < species) & (srow < species), ub[...], 0.0)
    zb[...] = jnp.zeros(zb.shape, F32)
    zb[0:SP] = half
    half = zb[...]
    gram = half + half.T

    def round_(i, w):
        w = jnp.dot(w, gram, precision=HIGH, preferred_element_type=F32)
        return orth(orth(w, ranks), ranks)

    w = lax.fori_loop(0, ITERS, round_, w)

    whigh = w.astype(BF16).astype(F32)
    lhs = jnp.concatenate([whigh + pltpu.roll(whigh, SP, 1), w - whigh], axis=0).astype(BF16)
    lhs = lhs[:, 0 : 2 * SP]
    cflat = core.reshape(ranks * cx * YP, cz)

    def project(x):
        for g in range(cy // step):
            at = (x * (cy // step) + g) * wide
            out = jnp.dot(lhs, hl[:, at : at + wide], preferred_element_type=F32)
            out = out[0:ranks] + out[ranks:]
            for k in range(step):
                cflat[pl.ds(x * YP + g * step + k, ranks, stride=cx * YP), :] = (
                    out[:, k * cz : (k + 1) * cz]
                )

    hx = cx // 2
    for x in range(hx):
        project(x)
    first0 = []
    for d in range(1, nx):
        there = lax.rem(mx + d, nx)
        first0.append(send(core.at[:, there, 0:hx, 0:cy, :], mid0.at[:, :, mx, 0:cy, :], to_x(d)))
    for x in range(hx, cx):
        project(x)
    first1 = []
    for d in range(1, ny):
        there = lax.rem(my + d, ny)
        first1.append(send(core.at[there, :, hx:cx, 0:cy, :], mid1.at[:, :, my, 0:cy, :], to_y(d)))
    mid0[:, :, mx] = core[:, mx, 0:hx]
    mid1[:, :, my] = core[my, :, hx:cx]
    both_out[48:64] = w
    for copy in first0:
        copy.wait()
    second = []
    for d in range(1, ny):
        there = lax.rem(my + d, ny)
        second.append(send(mid0.at[there, :, :, 0:cy, :], recv.at[0:hx, my, :, 0:cy, :], to_y(d)))
    recv[0:hx, my] = mid0[my]
    for copy in first1:
        copy.wait()
    for d in range(1, nx):
        there = lax.rem(mx + d, nx)
        second.append(send(mid1.at[there, :, :, 0:cy, :], recv.at[hx:cx, :, mx, 0:cy, :], to_x(d)))
    recv[hx:cx, :, mx] = mid1[mx]
    for copy in second:
        copy.wait()

    rows = ny * nx * YP
    for x in range(cx):
        high, low = split(recv[x].reshape(rows, cz))
        ah[:, :, :, x * cz : (x + 1) * cz] = high.reshape(nz, ns, YP, cz)
        al[:, :, :, x * cz : (x + 1) * cz] = low.reshape(nz, ns, YP, cz)
    depth = cx * cz
    columns = nz * YP
    lrows = ah.reshape(ny, nx * YP, depth), al.reshape(ny, nx * YP, depth)

    def gram_rows(y, side):
        lh, ll = lrows[0][y], lrows[1][y]
        rh, rl = ah[:, side].reshape(columns, depth), al[:, side].reshape(columns, depth)
        out = (
            lax.dot_general(lh, rh, NT, preferred_element_type=F32)
            + lax.dot_general(lh, rl, NT, preferred_element_type=F32)
            + lax.dot_general(ll, rh, NT, preferred_element_type=F32)
        )
        return out.reshape(nx, YP, columns)

    hy = YP // 2
    order = [lax.rem(my + t, ny) for t in range(1, ny)] + [my]
    swaps, first0, first1 = [], [], []

    def theirs(t):
        y = order[t]
        gs[y] = gram_rows(y, 1 - sa)
        swaps.append(send(gs.at[y], gr.at[y], to_sa(1)))

    def ours(t):
        y = order[t]
        mine = gram_rows(y, sa)
        swaps[t].wait()
        go[y] = mine + gr[y]
        for d in range(1, nx):
            there = lax.rem(mx + d, nx)
            first0.append(send(go.at[y, there, 0:hy, :], r1a.at[d - 1, y], to_x(d)))
        if t < ny - 1:
            first1.append(send(go.at[y, :, hy:YP, :], r1b.at[t], to_y(t + 1)))

    theirs(0)
    for t in range(1, ny):
        theirs(t)
        ours(t - 1)
    ours(ny - 1)
    for copy in first0:
        copy.wait()
    out = go[:, mx, 0:hy, :]
    for d in range(1, nx):
        out = out + r1a[d - 1]
    t0[...] = out
    second0 = []
    for d in range(1, ny):
        second0.append(send(t0.at[lax.rem(my + d, ny)], r2a.at[d - 1], to_y(d)))
    for copy in first1:
        copy.wait()
    out = go[my, :, hy:YP, :]
    for d in range(1, ny):
        out = out + r1b[d - 1]
    t1[...] = out
    second1 = []
    for d in range(1, nx):
        second1.append(send(t1.at[lax.rem(mx + d, nx)], r2b.at[d - 1], to_x(d)))
    for copy in second0:
        copy.wait()
    out = t0[my]
    for d in range(1, ny):
        out = out + r2a[d - 1]
    hb[0:hy, 0 : nz * YP] = out
    for copy in second1:
        copy.wait()
    out = t1[mx]
    for d in range(1, nx):
        out = out + r2b[d - 1]
    hb[hy:YP, 0 : nz * YP] = out

    lane = lax.broadcasted_iota(jnp.int32, (16, LANES), 1)
    for g in range(nz):
        tile = (g * YP) // LANES
        at = g * YP - tile * LANES
        parts = []
        for part in (hb[0:16], hb[16:32], hb[32:48]):
            piece = part[:, tile * LANES : (tile + 1) * LANES]
            if at:
                piece = pltpu.roll(piece, LANES - at, 1)
            if at + YP > LANES:
                other = part[:, (tile + 1) * LANES : (tile + 2) * LANES]
                piece = jnp.where(lane < LANES - at, piece, pltpu.roll(other, LANES - at, 1))
            parts.append(piece)
        moved = jnp.where(lane < 2 * cy, pltpu.roll(parts[1], cy, 1), pltpu.roll(parts[2], 2 * cy, 1))
        pack[g] = jnp.where(lane < cy, parts[0], moved)
    last = []
    for d in range(1, nz):
        last.append(send(pack.at[lax.rem(gx + d, nz)], r3.at[d - 1], to_z(d)))
    out = pack[gx]
    for copy in last:
        copy.wait()
    for d in range(1, nz):
        out = out + r3[d - 1]
    out = out * (1.0 / cfg["terms"])
    both_out[0:16] = out
    both_out[16:32] = pltpu.roll(out, LANES - cy, 1)
    both_out[32:48] = pltpu.roll(out, LANES - 2 * cy, 1)


def tail(species, cy, both, basis, block):
    basis[...] = both[48:64, 0:species]
    block[...] = both[0:cy, 0:cy]


def on_device(cfg, field, start):
    species, cx, cy, cz = field.shape
    ranks = start.shape[1]
    nx, ny, nz = cfg["nx"], cfg["ny"], cfg["nz"]
    cols = nz * YP
    colsp = -(-cols // LANES) * LANES
    hy = YP // 2
    hx = cx // 2
    cells = cx * cy * cz
    copies = 1 + nx * ny - 1 + nz - 1 + 2 * (nx + ny - 2) + ny + ny * (nx - 1) + ny - 1 + nx + ny - 2 + nz - 1
    vmem = pltpu.VMEM
    scratch = [
        vmem((SP, cx * cy, cz), F32), vmem((2 * SP, cells), BF16), vmem((SP, LANES), F32),
        vmem((LANES, LANES), F32), vmem((ranks, LANES), F32), vmem((2, 16, LANES), F32), vmem((nx * ny, 16, LANES), F32), vmem((nz, 16, LANES), F32),
        vmem((ny, nx, cx, YP, cz), F32), vmem((ny, hx, nx, YP, cz), F32),
        vmem((nx, hx, ny, YP, cz), F32), vmem((cx, ny, nx, YP, cz), F32),
        vmem((nz, 2, YP, cx * cz), BF16), vmem((nz, 2, YP, cx * cz), BF16),
        vmem((ny, nx, YP, cols), F32), vmem((ny, nx, YP, cols), F32), vmem((ny, nx, YP, cols), F32),
        vmem((nx - 1, ny, hy, cols), F32), vmem((ny - 1, nx, hy, cols), F32),
        vmem((ny, hy, cols), F32), vmem((nx, hy, cols), F32),
        vmem((ny - 1, hy, cols), F32), vmem((nx - 1, hy, cols), F32),
        vmem((YP, colsp), F32), vmem((nz, 16, LANES), F32), vmem((nz - 1, 16, LANES), F32),
        pltpu.SemaphoreType.DMA, pltpu.SemaphoreType.DMA((copies,)), pltpu.SemaphoreType.DMA((copies,)),
    ]
    both = pl.pallas_call(
        functools.partial(kernel, cfg),
        out_shape=jax.ShapeDtypeStruct((64, LANES), F32),
        in_specs=[pl.BlockSpec(memory_space=pl.ANY), pl.BlockSpec(memory_space=vmem)],
        out_specs=pl.BlockSpec(memory_space=vmem),
        scratch_shapes=scratch,
        compiler_params=pltpu.CompilerParams(
            collective_id=0, has_side_effects=True, vmem_limit_bytes=56 * 1024 * 1024
        ),
        name="tucker_step",
    )(field.transpose(0, 2, 1, 3).reshape(species, cx * cy, cz), start.T)
    basis, block = pl.pallas_call(
        functools.partial(tail, species, cy),
        out_shape=(
            jax.ShapeDtypeStruct((ranks, species), F32),
            jax.ShapeDtypeStruct((cy, cy), F32),
        ),
        in_specs=[pl.BlockSpec(memory_space=vmem)],
        out_specs=(pl.BlockSpec(memory_space=vmem), pl.BlockSpec(memory_space=vmem)),
        name="parts",
    )(both)
    return basis.T, block


def solution(mesh):
    nz, n_plane, ns = mesh.shape["gx"], mesh.shape["gy"], mesh.shape["sa"]
    nx = math.isqrt(n_plane)
    cfg = dict(nx=nx, ny=n_plane // nx, nz=nz)

    def run(field, start):
        species, cx, cy, cz = field.shape
        ranks = start.shape[1]
        total = cx * nz * cz * ns
        full = dict(cfg, cx=cx, cy=cy, step=14 if cy % 14 == 0 else cy, cells=total * cy * n_plane, terms=ranks * total)
        return on_device(full, field, start)

    return jax.shard_map(
        run, mesh=mesh, in_specs=(P(None, "gx", "gy", "sa"), P()),
        out_specs=(P(), P("gy", ("gx", "sa"))), check_vma=False,
    )
```

```python
import functools
import math

import jax
import jax.numpy as jnp
from jax import lax
from jax.experimental import pallas as pl
from jax.experimental.pallas import tpu as pltpu
from jax.sharding import PartitionSpec as P

ITERS = 4
F32 = jnp.float32
BF16 = jnp.bfloat16
HIGH = lax.Precision.HIGHEST
LANES = 128
SP = 48
YP = 48
NT = (((1,), (1,)), ((), ()))


def split(value):
    high = value.astype(BF16)
    return high, (value - high.astype(F32)).astype(BF16)


def orth(w, ranks):
    products = (w[:, None, :] * w[None, :, :]).reshape(ranks * ranks, LANES)
    first, rest = split(products)
    second, third = split(products - first.astype(F32))
    ones = jnp.ones((LANES, LANES), BF16)
    inner = (
        jnp.dot(first, ones, preferred_element_type=F32)
        + jnp.dot(second, ones, preferred_element_type=F32)
        + jnp.dot(third, ones, preferred_element_type=F32)
    )
    lines = [inner[i * ranks : (i + 1) * ranks] for i in range(ranks)]
    row = lax.broadcasted_iota(jnp.int32, (ranks, LANES), 0)
    pivots = jnp.ones((ranks, LANES), F32)
    for j in range(ranks):
        line = lines[j]
        pivots = jnp.where(row == j, line, pivots)
        factor = line * (1.0 / line[j : j + 1])
        if j + 1 < ranks:
            below = jnp.where(row > j, factor, 0.0)
            w = w - below * w[j : j + 1]
            for i in range(j + 1, ranks):
                lines[i] = lines[i] - factor[i : i + 1] * line
    return w * lax.rsqrt(pivots)


def kernel(cfg, field, start, both_out, fv, hl, ub, zb, wb, b_sa, b_p, b_z,
           core, mid0, mid1, recv, ah, al, gs, go, gr, r1a, r1b, t0, t1, r2a, r2b, hb, pack, r3,
           load_sem, ssem, rsem):
    nx, ny, nz, ns = cfg["nx"], cfg["ny"], cfg["nz"], 2
    species, cz = field.shape[0], field.shape[2]
    cx, cy = cfg["cx"], cfg["cy"]
    ranks = start.shape[0]
    gx, gy, sa = lax.axis_index("gx"), lax.axis_index("gy"), lax.axis_index("sa")
    mx, my = lax.rem(gy, nx), gy // nx

    def to_sa(d):
        return {"sa": 1 - sa}

    def to_x(d):
        return {"gy": my * nx + lax.rem(mx + d, nx)}

    def to_y(d):
        return {"gy": lax.rem(my + d, ny) * nx + mx}

    def to_plane(d):
        return {"gy": lax.rem(my + d // nx, ny) * nx + lax.rem(mx + d % nx, nx)}

    def to_z(d):
        return {"gx": lax.rem(gx + d, nz)}

    used = [0]

    def send(src, dst, target):
        k = used[0]
        used[0] += 1
        copy = pltpu.make_async_remote_copy(
            src_ref=src, dst_ref=dst, send_sem=ssem.at[k], recv_sem=rsem.at[k],
            device_id=target, device_id_type=pl.DeviceIdType.MESH,
        )
        copy.start()
        return copy

    step = cfg["step"]
    groups = cy // step
    loads = []
    for g in range(groups):
        part = pl.ds(g * step * cx, step * cx)
        loads.append(pltpu.make_async_copy(field.at[:, part], fv.at[0:species, part], load_sem.at[g]))
        loads[g].start()
    barrier = pltpu.get_barrier_semaphore()
    peers = [to_sa(1)] + [to_plane(d) for d in range(1, nx * ny)]
    peers += [to_z(d) for d in range(1, nz)]
    for peer in peers:
        pl.semaphore_signal(barrier, inc=1, device_id=peer, device_id_type=pl.DeviceIdType.MESH)
    fv[species:SP] = jnp.zeros((SP - species, cx * cy, cz), F32)
    ub[...] = jnp.zeros(ub.shape, F32)
    wb[...] = jnp.zeros(wb.shape, F32)
    wb[:, 0:species] = start[...]

    flat = fv.reshape(SP * cx * cy, cz)
    wide = step * cz
    total = jnp.zeros((2 * SP, 2 * SP), F32)
    for g in range(groups):
        loads[g].wait()
        for x in range(cx):
            cols = [flat[pl.ds((g * step + k) * cx + x, SP, stride=cx * cy), :] for k in range(step)]
            high, low = split(jnp.concatenate(cols, axis=1))
            both = jnp.concatenate([high, low], axis=0)
            at = (x * groups + g) * wide
            hl[:, at : at + wide] = both
            total = total + lax.dot_general(both, both, NT, preferred_element_type=F32)
    ub[:, 0 : 2 * SP] = total
    full = ub[0:SP] + ub[SP:] + pltpu.roll(ub[0:SP], LANES - SP, 1)
    lane = lax.broadcasted_iota(jnp.int32, (8, LANES), 1)
    starts = range(0, species, 8)
    shifts = [sum(species - a for a in starts[:b]) - at for b, at in enumerate(starts)]
    packed = jnp.zeros((8, LANES), F32)
    for at, shift in zip(starts, shifts):
        rows = jnp.where((lane >= at) & (lane < species), full[at : at + 8], 0.0)
        packed = packed + (pltpu.roll(rows, shift, 1) if shift else rows)

    pl.semaphore_wait(barrier, len(peers))

    def start_sum(value, buf, n, me, target):
        buf[me] = value
        return [send(buf.at[me], buf.at[me], target(d)) for d in range(1, n)]

    def end_sum(copies, buf, n):
        for copy in copies:
            copy.wait()
        out = buf[0]
        for k in range(1, n):
            out = out + buf[k]
        return out

    packed = end_sum(start_sum(packed, b_sa, ns, sa, to_sa), b_sa, ns)
    packed = end_sum(start_sum(packed, b_p, nx * ny, gy, to_plane), b_p, nx * ny)
    copies = start_sum(packed, b_z, nz, gx, to_z)
    w = wb[...]
    w = orth(orth(w, ranks), ranks)
    packed = end_sum(copies, b_z, nz)

    scale = 1.0 / cfg["cells"]
    packed = packed * scale
    zb[...] = jnp.zeros(zb.shape, F32)
    for at, shift in zip(starts, shifts):
        rows = pltpu.roll(packed, LANES - shift, 1) if shift else packed
        zb[at : at + 8] = jnp.where((lane >= at) & (lane < species), rows, 0.0)
    upper = zb[...]
    row = lax.broadcasted_iota(jnp.int32, zb.shape, 0)
    column = lax.broadcasted_iota(jnp.int32, zb.shape, 1)
    gram = upper + jnp.where(column >= (row & ~7) + 8, upper, 0.0).T

    def round_(i, w):
        w = jnp.dot(w, gram, precision=HIGH, preferred_element_type=F32)
        return orth(orth(w, ranks), ranks)

    w = lax.fori_loop(0, ITERS, round_, w)

    whigh = w.astype(BF16).astype(F32)
    lhs = jnp.concatenate([whigh + pltpu.roll(whigh, SP, 1), w - whigh], axis=0).astype(BF16)
    lhs = lhs[:, 0 : 2 * SP]
    cflat = core.reshape(ranks * cx * YP, cz)

    def project(x):
        for g in range(groups):
            at = (x * groups + g) * wide
            out = jnp.dot(lhs, hl[:, at : at + wide], preferred_element_type=F32)
            out = out[0:ranks] + out[ranks:]
            for k in range(step):
                cflat[pl.ds(x * YP + g * step + k, ranks, stride=cx * YP), :] = (
                    out[:, k * cz : (k + 1) * cz]
                )

    hx = cx // 2
    firsts = {}
    for a in range(hx):
        project(a)
        firsts[a] = []
        for d in range(1, nx):
            there = lax.rem(mx + d, nx)
            firsts[a].append(send(core.at[:, there, a, 0:cy], mid0.at[a, :, mx, 0:cy], to_x(d)))
        x = hx + a
        project(x)
        firsts[x] = []
        for d in range(1, ny):
            there = lax.rem(my + d, ny)
            firsts[x].append(send(core.at[there, :, x, 0:cy], mid1.at[a, :, my, 0:cy], to_y(d)))
    for a in range(hx):
        mid0[a, :, mx] = core[:, mx, a]
        mid1[a, :, my] = core[my, :, hx + a]
    both_out[48:64] = w
    seconds = {}
    for a in range(hx):
        for copy in firsts[a]:
            copy.wait()
        seconds[a] = []
        for d in range(1, ny):
            there = lax.rem(my + d, ny)
            seconds[a].append(send(mid0.at[a, there, :, 0:cy], recv.at[a, my, :, 0:cy], to_y(d)))
        recv[a, my] = mid0[a, my]
        x = hx + a
        for copy in firsts[x]:
            copy.wait()
        seconds[x] = []
        for d in range(1, nx):
            there = lax.rem(mx + d, nx)
            seconds[x].append(send(mid1.at[a, there, :, 0:cy], recv.at[x, :, mx, 0:cy], to_x(d)))
        recv[x, :, mx] = mid1[a, mx]

    rows = ny * nx * YP
    for x in [k for a in range(hx) for k in (a, hx + a)]:
        for copy in seconds[x]:
            copy.wait()
        high, low = split(recv[x].reshape(rows, cz))
        ah[:, :, :, x * cz : (x + 1) * cz] = high.reshape(nz, ns, YP, cz)
        al[:, :, :, x * cz : (x + 1) * cz] = low.reshape(nz, ns, YP, cz)
    depth = cx * cz
    columns = nz * YP
    lrows = ah.reshape(ny, nx * YP, depth), al.reshape(ny, nx * YP, depth)

    def gram_rows(y, side):
        lh, ll = lrows[0][y], lrows[1][y]
        rh, rl = ah[:, side].reshape(columns, depth), al[:, side].reshape(columns, depth)
        out = (
            lax.dot_general(lh, rh, NT, preferred_element_type=F32)
            + lax.dot_general(lh, rl, NT, preferred_element_type=F32)
            + lax.dot_general(ll, rh, NT, preferred_element_type=F32)
        )
        return out.reshape(nx, YP, columns)

    hy = YP // 2
    order = [lax.rem(my + t, ny) for t in range(1, ny)] + [my]
    swaps, first0, first1 = [], {}, {}

    def theirs(t):
        y = order[t]
        gs[y] = gram_rows(y, 1 - sa)
        swaps.append(send(gs.at[y], gr.at[y], to_sa(1)))

    def ours(t):
        y = order[t]
        mine = gram_rows(y, sa)
        swaps[t].wait()
        go[y] = mine + gr[y]
        for d in range(1, nx):
            there = lax.rem(mx + d, nx)
            first0[t, d] = send(go.at[y, there, 0:hy, :], r1a.at[d - 1, y], to_x(d))
        if t < ny - 1:
            for d in list(range(1, nx)) + [0]:
                there = lax.rem(mx + d, nx)
                first1[t, d] = send(go.at[y, there, hy:YP, :], r1b.at[t, there], to_y(t + 1))

    theirs(0)
    for t in range(1, ny):
        theirs(t)
        ours(t - 1)
    ours(ny - 1)
    def sum0(t):
        y = order[t]
        out = go[y, mx, 0:hy, :]
        for d in range(1, nx):
            first0[t, d].wait()
            out = out + r1a[d - 1, y]
        return out

    def sum1(d):
        there = lax.rem(mx + d, nx)
        out = go[my, there, hy:YP, :]
        for t in range(ny - 1):
            first1[t, d].wait()
            out = out + r1b[t, there]
        return out

    second0, second1 = [], []
    for k in range(max(nx, ny) - 1):
        if k < ny - 1:
            t0[k] = sum0(k)
            second0.append(send(t0.at[k], r2a.at[k], to_y(k + 1)))
        if k < nx - 1:
            t1[k] = sum1(k + 1)
            second1.append(send(t1.at[k], r2b.at[k], to_x(k + 1)))
    out0, out1 = sum0(ny - 1), sum1(0)
    for k in range(ny - 1):
        second0[k].wait()
        out0 = out0 + r2a[k]
    for k in range(nx - 1):
        second1[k].wait()
        out1 = out1 + r2b[k]
    hb[0:hy, 0 : nz * YP] = out0
    hb[hy:YP, 0 : nz * YP] = out1

    lane = lax.broadcasted_iota(jnp.int32, (16, LANES), 1)
    for g in range(nz):
        tile = (g * YP) // LANES
        at = g * YP - tile * LANES
        parts = []
        for part in (hb[0:16], hb[16:32], hb[32:48]):
            piece = part[:, tile * LANES : (tile + 1) * LANES]
            if at:
                piece = pltpu.roll(piece, LANES - at, 1)
            if at + YP > LANES:
                other = part[:, (tile + 1) * LANES : (tile + 2) * LANES]
                piece = jnp.where(lane < LANES - at, piece, pltpu.roll(other, LANES - at, 1))
            parts.append(piece)
        moved = jnp.where(lane < 2 * cy, pltpu.roll(parts[1], cy, 1), pltpu.roll(parts[2], 2 * cy, 1))
        pack[g] = jnp.where(lane < cy, parts[0], moved)
    last = []
    for d in range(1, nz):
        last.append(send(pack.at[lax.rem(gx + d, nz)], r3.at[d - 1], to_z(d)))
    out = pack[gx]
    for copy in last:
        copy.wait()
    for d in range(1, nz):
        out = out + r3[d - 1]
    out = out * (1.0 / cfg["terms"])
    both_out[0:16] = out
    both_out[16:32] = pltpu.roll(out, LANES - cy, 1)
    both_out[32:48] = pltpu.roll(out, LANES - 2 * cy, 1)


def tail(species, cy, both, basis, block):
    basis[...] = both[48:64, 0:species]
    block[...] = both[0:cy, 0:cy]


def on_device(cfg, field, start):
    species, cx, cy, cz = field.shape
    ranks = start.shape[1]
    nx, ny, nz = cfg["nx"], cfg["ny"], cfg["nz"]
    cols = nz * YP
    colsp = -(-cols // LANES) * LANES
    hy = YP // 2
    hx = cx // 2
    cells = cx * cy * cz
    ring = nx + ny - 2
    copies = 1 + nx * ny - 1 + nz - 1 + 2 * hx * ring + ny + 2 * nx * ny - nx - ny + nx * (ny - 1) + ring + nz
    vmem = pltpu.VMEM
    scratch = [
        vmem((SP, cx * cy, cz), F32), vmem((2 * SP, cells), BF16), vmem((2 * SP, LANES), F32),
        vmem((LANES, LANES), F32), vmem((ranks, LANES), F32), vmem((2, 8, LANES), F32), vmem((nx * ny, 8, LANES), F32), vmem((nz, 8, LANES), F32),
        vmem((ny, nx, cx, YP, cz), F32), vmem((hx, ny, nx, YP, cz), F32),
        vmem((hx, nx, ny, YP, cz), F32), vmem((cx, ny, nx, YP, cz), F32),
        vmem((nz, 2, YP, cx * cz), BF16), vmem((nz, 2, YP, cx * cz), BF16),
        vmem((ny, nx, YP, cols), F32), vmem((ny, nx, YP, cols), F32), vmem((ny, nx, YP, cols), F32),
        vmem((nx - 1, ny, hy, cols), F32), vmem((ny - 1, nx, hy, cols), F32),
        vmem((ny - 1, hy, cols), F32), vmem((nx - 1, hy, cols), F32),
        vmem((ny - 1, hy, cols), F32), vmem((nx - 1, hy, cols), F32),
        vmem((YP, colsp), F32), vmem((nz, 16, LANES), F32), vmem((nz - 1, 16, LANES), F32),
        pltpu.SemaphoreType.DMA((cfg["cy"] // cfg["step"],)), pltpu.SemaphoreType.DMA((copies,)), pltpu.SemaphoreType.DMA((copies,)),
    ]
    both = pl.pallas_call(
        functools.partial(kernel, cfg),
        out_shape=jax.ShapeDtypeStruct((64, LANES), F32),
        in_specs=[pl.BlockSpec(memory_space=pl.ANY), pl.BlockSpec(memory_space=vmem)],
        out_specs=pl.BlockSpec(memory_space=vmem),
        scratch_shapes=scratch,
        compiler_params=pltpu.CompilerParams(
            collective_id=0, has_side_effects=True, vmem_limit_bytes=56 * 1024 * 1024
        ),
        name="tucker_step",
    )(field.transpose(0, 2, 1, 3).reshape(species, cx * cy, cz), start.T)
    basis, block = pl.pallas_call(
        functools.partial(tail, species, cy),
        out_shape=(
            jax.ShapeDtypeStruct((ranks, species), F32),
            jax.ShapeDtypeStruct((cy, cy), F32),
        ),
        in_specs=[pl.BlockSpec(memory_space=vmem)],
        out_specs=(pl.BlockSpec(memory_space=vmem), pl.BlockSpec(memory_space=vmem)),
        name="parts",
    )(both)
    return basis.T, block


def solution(mesh):
    nz, n_plane, ns = mesh.shape["gx"], mesh.shape["gy"], mesh.shape["sa"]
    nx = math.isqrt(n_plane)
    cfg = dict(nx=nx, ny=n_plane // nx, nz=nz)

    def run(field, start):
        species, cx, cy, cz = field.shape
        ranks = start.shape[1]
        total = cx * nz * cz * ns
        full = dict(cfg, cx=cx, cy=cy, step=14 if cy % 14 == 0 else cy, cells=total * cy * n_plane, terms=ranks * total)
        return on_device(full, field, start)

    return jax.shard_map(
        run, mesh=mesh, in_specs=(P(None, "gx", "gy", "sa"), P()),
        out_specs=(P(), P("gy", ("gx", "sa"))), check_vma=False,
    )
```

```python
import functools
import math

import jax
import jax.numpy as jnp
from jax import lax
from jax.experimental import pallas as pl
from jax.experimental.pallas import tpu as pltpu
from jax.sharding import PartitionSpec as P

ITERS = 4
F32 = jnp.float32
BF16 = jnp.bfloat16
HIGH = lax.Precision.HIGHEST
LANES = 128
SP = 48
YP = 48
NT = (((1,), (1,)), ((), ()))


def split(value):
    high = value.astype(BF16)
    return high, (value - high.astype(F32)).astype(BF16)


def orth(w, ranks):
    products = (w[:, None, :] * w[None, :, :]).reshape(ranks * ranks, LANES)
    first, rest = split(products)
    second, third = split(products - first.astype(F32))
    ones = jnp.ones((LANES, LANES), BF16)
    inner = (
        jnp.dot(first, ones, preferred_element_type=F32)
        + jnp.dot(second, ones, preferred_element_type=F32)
        + jnp.dot(third, ones, preferred_element_type=F32)
    )
    lines = [inner[i * ranks : (i + 1) * ranks] for i in range(ranks)]
    row = lax.broadcasted_iota(jnp.int32, (ranks, LANES), 0)
    pivots = jnp.ones((ranks, LANES), F32)
    for j in range(ranks):
        line = lines[j]
        pivots = jnp.where(row == j, line, pivots)
        factor = line * (1.0 / line[j : j + 1])
        if j + 1 < ranks:
            below = jnp.where(row > j, factor, 0.0)
            w = w - below * w[j : j + 1]
            for i in range(j + 1, ranks):
                lines[i] = lines[i] - factor[i : i + 1] * line
    return w * lax.rsqrt(pivots)


def kernel(cfg, field, start, both_out, fv, hl, ub, zb, wb, b_sa, b_p, b_z,
           ft, raw, own_a, cd, ca, recv_d, recv_a, ah, al, gs, go, gr, r1a, r1b, t0, t1, r2a, r2b, hb, pack, r3,
           load_sem, ssem, rsem):
    nx, ny, nz, ns = cfg["nx"], cfg["ny"], cfg["nz"], 2
    species, cz = field.shape[0], field.shape[2]
    cx, cy = cfg["cx"], cfg["cy"]
    ranks = start.shape[0]
    gx, gy, sa = lax.axis_index("gx"), lax.axis_index("gy"), lax.axis_index("sa")
    mx, my = lax.rem(gy, nx), gy // nx

    def to_sa(d):
        return {"sa": 1 - sa}

    def to_x(d):
        return {"gy": my * nx + lax.rem(mx + d, nx)}

    def to_y(d):
        return {"gy": lax.rem(my + d, ny) * nx + mx}

    def to_plane(d):
        return {"gy": lax.rem(my + d // nx, ny) * nx + lax.rem(mx + d % nx, nx)}

    p = (1 - sa) * mx + sa * my
    q = (1 - sa) * my + sa * mx

    def to_first(d):
        there = lax.rem(p + d, nx)
        return {"gy": (1 - sa) * (q * nx + there) + sa * (there * nx + q)}

    def to_second(d):
        there = lax.rem(q + d, ny)
        return {"gy": (1 - sa) * (there * nx + p) + sa * (p * nx + there)}

    def to_z(d):
        return {"gx": lax.rem(gx + d, nz)}

    used = [0]

    def send(src, dst, target):
        k = used[0]
        used[0] += 1
        copy = pltpu.make_async_remote_copy(
            src_ref=src, dst_ref=dst, send_sem=ssem.at[k], recv_sem=rsem.at[k],
            device_id=target, device_id_type=pl.DeviceIdType.MESH,
        )
        copy.start()
        return copy

    hy = YP // 2
    groups = [(0, hy // 2), (hy // 2, hy // 2), (hy, cy - hy)]
    loads = []
    for g, (y0, n) in enumerate(groups):
        part = pl.ds(y0 * cx, n * cx)
        loads.append(pltpu.make_async_copy(field.at[:, part], fv.at[0:species, part], load_sem.at[g]))
        loads[g].start()
    barrier = pltpu.get_barrier_semaphore()
    peers = [to_sa(1)] + [to_plane(d) for d in range(1, nx * ny)]
    peers += [to_z(d) for d in range(1, nz)]
    for peer in peers:
        pl.semaphore_signal(barrier, inc=1, device_id=peer, device_id_type=pl.DeviceIdType.MESH)
    fv[species:SP] = jnp.zeros((SP - species, cx * cy, cz), F32)
    ub[...] = jnp.zeros(ub.shape, F32)
    wb[...] = jnp.zeros(wb.shape, F32)
    wb[:, 0:species] = start[...]

    flat = fv.reshape(SP * cx * cy, cz)
    total = jnp.zeros((2 * SP, 2 * SP), F32)
    wide = (cy - hy) * cz
    for g, (y0, n) in enumerate(groups):
        loads[g].wait()
        for x in range(cx):
            cols = [flat[pl.ds((y0 + k) * cx + x, SP, stride=cx * cy), :] for k in range(n)]
            if y0 < hy:
                for k in range(n):
                    ft[x, y0 + k] = cols[k]
            high, low = split(jnp.concatenate(cols, axis=1))
            both = jnp.concatenate([high, low], axis=0)
            if y0 >= hy:
                hl[:, x * wide : (x + 1) * wide] = both
            total = total + lax.dot_general(both, both, NT, preferred_element_type=F32)
    ub[:, 0 : 2 * SP] = total
    full = ub[0:SP] + ub[SP:] + pltpu.roll(ub[0:SP], LANES - SP, 1)
    lane = lax.broadcasted_iota(jnp.int32, (8, LANES), 1)
    starts = range(0, species, 8)
    shifts = [sum(species - a for a in starts[:b]) - at for b, at in enumerate(starts)]
    packed = jnp.zeros((8, LANES), F32)
    for at, shift in zip(starts, shifts):
        rows = jnp.where((lane >= at) & (lane < species), full[at : at + 8], 0.0)
        packed = packed + (pltpu.roll(rows, shift, 1) if shift else rows)

    pl.semaphore_wait(barrier, len(peers))

    def start_sum(value, buf, n, me, target):
        buf[me] = value
        return [send(buf.at[me], buf.at[me], target(d)) for d in range(1, n)]

    def end_sum(copies, buf, n):
        for copy in copies:
            copy.wait()
        out = buf[0]
        for k in range(1, n):
            out = out + buf[k]
        return out

    packed = end_sum(start_sum(packed, b_sa, ns, sa, to_sa), b_sa, ns)
    packed = end_sum(start_sum(packed, b_p, nx * ny, gy, to_plane), b_p, nx * ny)
    copies = start_sum(packed, b_z, nz, gx, to_z)
    bulk = {}
    for d in range(1, nx):
        there = lax.rem(p + d, nx)
        bulk[d] = send(ft.at[there, :, 0:species], raw.at[d - 1, :, 0:species], to_first(d))
    w = wb[...]
    w = orth(orth(w, ranks), ranks)
    packed = end_sum(copies, b_z, nz)

    scale = 1.0 / cfg["cells"]
    packed = packed * scale
    zb[...] = jnp.zeros(zb.shape, F32)
    for at, shift in zip(starts, shifts):
        rows = pltpu.roll(packed, LANES - shift, 1) if shift else packed
        zb[at : at + 8] = jnp.where((lane >= at) & (lane < species), rows, 0.0)
    upper = zb[...]
    row = lax.broadcasted_iota(jnp.int32, zb.shape, 0)
    column = lax.broadcasted_iota(jnp.int32, zb.shape, 1)
    gram = upper + jnp.where(column >= (row & ~7) + 8, upper, 0.0).T

    def round_(i, w):
        w = jnp.dot(w, gram, precision=HIGH, preferred_element_type=F32)
        return orth(orth(w, ranks), ranks)

    w = lax.fori_loop(0, ITERS, round_, w)

    whigh = w.astype(BF16).astype(F32)
    lhs = jnp.concatenate([whigh + pltpu.roll(whigh, SP, 1), w - whigh], axis=0).astype(BF16)
    lhs = lhs[:, 0 : 2 * SP]
    rg = ranks // ny
    aflat = own_a.reshape(ranks * cx * hy, cz)
    dflat = cd.reshape(ranks * nx * hy, cz)
    cd4, ca4 = cd.reshape(ny, rg, nx, hy, cz), ca.reshape(ny, rg, nx, hy, cz)
    srow = lax.broadcasted_iota(jnp.int32, (SP, cz), 0)

    def project(both):
        out = jnp.dot(lhs, both, preferred_element_type=F32)
        return out[0:ranks] + out[ranks:]

    def project_raw(d):
        n = hy // 2
        for h in range(0, hy, n):
            if d:
                tiles = [jnp.where(srow < species, raw[d - 1, h + k], 0.0) for k in range(n)]
            else:
                tiles = [ft[p, h + k] for k in range(n)]
            high, low = split(jnp.concatenate(tiles, axis=1))
            out = project(jnp.concatenate([high, low], axis=0))
            for k in range(n):
                dflat[pl.ds(d * hy + h + k, ranks, stride=nx * hy), :] = out[:, k * cz : (k + 1) * cz]

    low_rows = cy - hy
    for x in range(cx):
        out = project(hl[:, x * wide : (x + 1) * wide])
        for k in range(low_rows):
            aflat[pl.ds(x * hy + k, ranks, stride=cx * hy), :] = out[:, k * cz : (k + 1) * cz]
    firsts = []
    for d in range(1, nx):
        there = lax.rem(p + d, nx)
        firsts.append(send(own_a.at[:, there, 0:low_rows], ca.at[:, d, 0:low_rows], to_first(d)))
    seconds = []
    for d in [0] + sorted(range(1, nx), key=lambda d: min(d, nx - d)):
        if d:
            bulk[d].wait()
        project_raw(d)
        for e in range(1, ny):
            there = lax.rem(q + e, ny)
            seconds.append(send(cd4.at[there, :, d], recv_d.at[e - 1, :, d], to_second(e)))
    ca[:, 0] = own_a[:, p]
    both_out[48:64] = w
    for copy in firsts:
        copy.wait()
    for e in range(1, ny):
        there = lax.rem(q + e, ny)
        seconds.append(
            send(ca4.at[there, :, :, 0:low_rows], recv_a.at[e - 1, :, :, 0:low_rows], to_second(e))
        )

    def place(e, d):
        above, below = lax.rem(q + ny - e, ny), lax.rem(p + nx - d, nx)
        block = (1 - sa) * (above * nx + below) + sa * (below * nx + above)
        parts = []
        for r in range(rg):
            top = recv_d[e - 1, r, d] if e else cd4[q, r, d]
            end = recv_a[e - 1, r, d] if e else ca4[q, r, d]
            parts.append(jnp.concatenate([top, end], axis=0))
        high, low = split(jnp.concatenate(parts, axis=1))
        ah[block // ns, lax.rem(block, ns)] = high
        al[block // ns, lax.rem(block, ns)] = low

    for d in range(nx):
        place(0, d)
    for copy in seconds:
        copy.wait()
    for e in range(1, ny):
        for d in range(nx):
            place(e, d)
    depth = rg * cz
    columns = nz * YP
    lrows = ah.reshape(ny, nx * YP, depth), al.reshape(ny, nx * YP, depth)

    def gram_rows(y, side):
        lh, ll = lrows[0][y], lrows[1][y]
        rh, rl = ah[:, side].reshape(columns, depth), al[:, side].reshape(columns, depth)
        out = (
            lax.dot_general(lh, rh, NT, preferred_element_type=F32)
            + lax.dot_general(lh, rl, NT, preferred_element_type=F32)
            + lax.dot_general(ll, rh, NT, preferred_element_type=F32)
        )
        return out.reshape(nx, YP, columns)

    order = [lax.rem(my + t, ny) for t in range(1, ny)] + [my]
    swaps, first0, first1 = [], {}, {}

    def theirs(t):
        y = order[t]
        gs[y] = gram_rows(y, 1 - sa)
        swaps.append(send(gs.at[y], gr.at[y], to_sa(1)))

    def ours(t):
        y = order[t]
        mine = gram_rows(y, sa)
        swaps[t].wait()
        go[y] = mine + gr[y]
        for d in range(1, nx):
            there = lax.rem(mx + d, nx)
            first0[t, d] = send(go.at[y, there, 0:hy, :], r1a.at[d - 1, y], to_x(d))
        if t < ny - 1:
            for d in list(range(1, nx)) + [0]:
                there = lax.rem(mx + d, nx)
                first1[t, d] = send(go.at[y, there, hy:YP, :], r1b.at[t, there], to_y(t + 1))

    theirs(0)
    for t in range(1, ny):
        theirs(t)
        ours(t - 1)
    ours(ny - 1)
    def sum0(t):
        y = order[t]
        out = go[y, mx, 0:hy, :]
        for d in range(1, nx):
            first0[t, d].wait()
            out = out + r1a[d - 1, y]
        return out

    def sum1(d):
        there = lax.rem(mx + d, nx)
        out = go[my, there, hy:YP, :]
        for t in range(ny - 1):
            first1[t, d].wait()
            out = out + r1b[t, there]
        return out

    second0, second1 = [], []
    for k in range(max(nx, ny) - 1):
        if k < ny - 1:
            t0[k] = sum0(k)
            second0.append(send(t0.at[k], r2a.at[k], to_y(k + 1)))
        if k < nx - 1:
            t1[k] = sum1(k + 1)
            second1.append(send(t1.at[k], r2b.at[k], to_x(k + 1)))
    out0, out1 = sum0(ny - 1), sum1(0)
    for k in range(ny - 1):
        second0[k].wait()
        out0 = out0 + r2a[k]
    for k in range(nx - 1):
        second1[k].wait()
        out1 = out1 + r2b[k]
    hb[0:hy, 0 : nz * YP] = out0
    hb[hy:YP, 0 : nz * YP] = out1

    lane = lax.broadcasted_iota(jnp.int32, (16, LANES), 1)
    for g in range(nz):
        tile = (g * YP) // LANES
        at = g * YP - tile * LANES
        parts = []
        for part in (hb[0:16], hb[16:32], hb[32:48]):
            piece = part[:, tile * LANES : (tile + 1) * LANES]
            if at:
                piece = pltpu.roll(piece, LANES - at, 1)
            if at + YP > LANES:
                other = part[:, (tile + 1) * LANES : (tile + 2) * LANES]
                piece = jnp.where(lane < LANES - at, piece, pltpu.roll(other, LANES - at, 1))
            parts.append(piece)
        moved = jnp.where(lane < 2 * cy, pltpu.roll(parts[1], cy, 1), pltpu.roll(parts[2], 2 * cy, 1))
        pack[g] = jnp.where(lane < cy, parts[0], moved)
    last = []
    for d in range(1, nz):
        last.append(send(pack.at[lax.rem(gx + d, nz)], r3.at[d - 1], to_z(d)))
    out = pack[gx]
    for copy in last:
        copy.wait()
    for d in range(1, nz):
        out = out + r3[d - 1]
    out = out * (1.0 / cfg["terms"])
    both_out[0:16] = out
    both_out[16:32] = pltpu.roll(out, LANES - cy, 1)
    both_out[32:48] = pltpu.roll(out, LANES - 2 * cy, 1)


def tail(species, cy, both, basis, block):
    basis[...] = both[48:64, 0:species]
    block[...] = both[0:cy, 0:cy]


def on_device(cfg, field, start):
    species, cx, cy, cz = field.shape
    ranks = start.shape[1]
    nx, ny, nz = cfg["nx"], cfg["ny"], cfg["nz"]
    cols = nz * YP
    colsp = -(-cols // LANES) * LANES
    hy = YP // 2
    depth = ranks // ny * cz
    ring = nx + ny - 2
    copies = 1 + nx * ny - 1 + nz - 1 + nx + nx + nx * ny + ny + ny + 2 * nx * ny - nx - ny + nx * (ny - 1) + ring + nz
    vmem = pltpu.VMEM
    scratch = [
        vmem((SP, cx * cy, cz), F32), vmem((2 * SP, cx * (cy - hy) * cz), BF16), vmem((2 * SP, LANES), F32),
        vmem((LANES, LANES), F32), vmem((ranks, LANES), F32), vmem((2, 8, LANES), F32), vmem((nx * ny, 8, LANES), F32), vmem((nz, 8, LANES), F32),
        vmem((cx, hy, SP, cz), F32), vmem((nx - 1, hy, SP, cz), F32),
        vmem((ranks, cx, hy, cz), F32), vmem((ranks, nx, hy, cz), F32), vmem((ranks, nx, hy, cz), F32),
        vmem((ny - 1, ranks // ny, nx, hy, cz), F32), vmem((ny - 1, ranks // ny, nx, hy, cz), F32),
        vmem((nz, 2, YP, depth), BF16), vmem((nz, 2, YP, depth), BF16),
        vmem((ny, nx, YP, cols), F32), vmem((ny, nx, YP, cols), F32), vmem((ny, nx, YP, cols), F32),
        vmem((nx - 1, ny, hy, cols), F32), vmem((ny - 1, nx, hy, cols), F32),
        vmem((ny - 1, hy, cols), F32), vmem((nx - 1, hy, cols), F32),
        vmem((ny - 1, hy, cols), F32), vmem((nx - 1, hy, cols), F32),
        vmem((YP, colsp), F32), vmem((nz, 16, LANES), F32), vmem((nz - 1, 16, LANES), F32),
        pltpu.SemaphoreType.DMA((3,)), pltpu.SemaphoreType.DMA((copies,)), pltpu.SemaphoreType.DMA((copies,)),
    ]
    both = pl.pallas_call(
        functools.partial(kernel, cfg),
        out_shape=jax.ShapeDtypeStruct((64, LANES), F32),
        in_specs=[pl.BlockSpec(memory_space=pl.ANY), pl.BlockSpec(memory_space=vmem)],
        out_specs=pl.BlockSpec(memory_space=vmem),
        scratch_shapes=scratch,
        compiler_params=pltpu.CompilerParams(
            collective_id=0, has_side_effects=True, vmem_limit_bytes=56 * 1024 * 1024
        ),
        name="tucker_step",
    )(field.transpose(0, 2, 1, 3).reshape(species, cx * cy, cz), start.T)
    basis, block = pl.pallas_call(
        functools.partial(tail, species, cy),
        out_shape=(
            jax.ShapeDtypeStruct((ranks, species), F32),
            jax.ShapeDtypeStruct((cy, cy), F32),
        ),
        in_specs=[pl.BlockSpec(memory_space=vmem)],
        out_specs=(pl.BlockSpec(memory_space=vmem), pl.BlockSpec(memory_space=vmem)),
        name="parts",
    )(both)
    return basis.T, block


def solution(mesh):
    nz, n_plane, ns = mesh.shape["gx"], mesh.shape["gy"], mesh.shape["sa"]
    nx = math.isqrt(n_plane)
    cfg = dict(nx=nx, ny=n_plane // nx, nz=nz)

    def run(field, start):
        species, cx, cy, cz = field.shape
        ranks = start.shape[1]
        total = cx * nz * cz * ns
        full = dict(cfg, cx=cx, cy=cy, cells=total * cy * n_plane, terms=ranks * total)
        return on_device(full, field, start)

    return jax.shard_map(
        run, mesh=mesh, in_specs=(P(None, "gx", "gy", "sa"), P()),
        out_specs=(P(), P("gy", ("gx", "sa"))), check_vma=False,
    )
```

```python
import functools
import math

import jax
import jax.numpy as jnp
from jax import lax
from jax.experimental import pallas as pl
from jax.experimental.pallas import tpu as pltpu
from jax.sharding import PartitionSpec as P

ITERS = 4
F32 = jnp.float32
BF16 = jnp.bfloat16
HIGH = lax.Precision.HIGHEST
LANES = 128
SP = 48
YP = 48
GROUP = 40
NT = (((1,), (1,)), ((), ()))


def split(value):
    high = value.astype(BF16)
    return high, (value - high.astype(F32)).astype(BF16)


def orth(w, ranks):
    products = (w[:, None, :] * w[None, :, :]).reshape(ranks * ranks, LANES)
    lane = lax.broadcasted_iota(jnp.int32, products.shape, 1)
    first = products.astype(BF16).astype(F32)
    rest = products - first
    second = rest.astype(BF16).astype(F32)
    pieces = jnp.where(lane < GROUP, first, jnp.where(lane < 2 * GROUP, second, rest - second))
    ones = jnp.ones((LANES, LANES), BF16)
    inner = jnp.dot(pieces.astype(BF16), ones, preferred_element_type=F32)
    lines = [inner[i * ranks : (i + 1) * ranks] for i in range(ranks)]
    row = lax.broadcasted_iota(jnp.int32, (ranks, LANES), 0)
    pivots = jnp.ones((ranks, LANES), F32)
    for j in range(ranks):
        line = lines[j]
        pivots = jnp.where(row == j, line, pivots)
        factor = line * (1.0 / line[j : j + 1])
        if j + 1 < ranks:
            below = jnp.where(row > j, factor, 0.0)
            w = w - below * w[j : j + 1]
            for i in range(j + 1, ranks):
                lines[i] = lines[i] - factor[i : i + 1] * line
    return w * lax.rsqrt(pivots)


def kernel(cfg, field, start, both_out, fv, hl, ub, zb, wb, b_sa, b_p, b_z,
           core, mid0, mid1, recv, ah, al, gs, go, gr, r1a, r1b, t0, t1, r2a, r2b, hb, pack, r3,
           load_sem, ssem, rsem):
    nx, ny, nz, ns = cfg["nx"], cfg["ny"], cfg["nz"], 2
    species, cz = field.shape[0], field.shape[2]
    cx, cy = cfg["cx"], cfg["cy"]
    ranks = start.shape[0]
    gx, gy, sa = lax.axis_index("gx"), lax.axis_index("gy"), lax.axis_index("sa")
    mx, my = lax.rem(gy, nx), gy // nx

    def to_sa(d):
        return {"sa": 1 - sa}

    def to_x(d):
        return {"gy": my * nx + lax.rem(mx + d, nx)}

    def to_y(d):
        return {"gy": lax.rem(my + d, ny) * nx + mx}

    def to_plane(d):
        return {"gy": lax.rem(my + d // nx, ny) * nx + lax.rem(mx + d % nx, nx)}

    def to_z(d):
        return {"gx": lax.rem(gx + d, nz)}

    used = [0]

    def send(src, dst, target):
        k = used[0]
        used[0] += 1
        copy = pltpu.make_async_remote_copy(
            src_ref=src, dst_ref=dst, send_sem=ssem.at[k], recv_sem=rsem.at[k],
            device_id=target, device_id_type=pl.DeviceIdType.MESH,
        )
        copy.start()
        return copy

    step = cfg["step"]
    groups = cy // step
    loads = []
    for g in range(groups):
        part = pl.ds(g * step * cx, step * cx)
        loads.append(pltpu.make_async_copy(field.at[:, part], fv.at[0:species, part], load_sem.at[g]))
        loads[g].start()
    barrier = pltpu.get_barrier_semaphore()
    peers = [to_sa(1)] + [to_plane(d) for d in range(1, nx * ny)]
    peers += [to_z(d) for d in range(1, nz)]
    for peer in peers:
        pl.semaphore_signal(barrier, inc=1, device_id=peer, device_id_type=pl.DeviceIdType.MESH)
    fv[species:SP] = jnp.zeros((SP - species, cx * cy, cz), F32)
    ub[...] = jnp.zeros(ub.shape, F32)
    wb[...] = jnp.zeros(wb.shape, F32)
    for c in range(3):
        wb[:, c * GROUP : c * GROUP + species] = start[...]

    flat = fv.reshape(SP * cx * cy, cz)
    wide = step * cz
    total = jnp.zeros((2 * SP, 2 * SP), F32)
    for g in range(groups):
        loads[g].wait()
        for x in range(cx):
            cols = [flat[pl.ds((g * step + k) * cx + x, SP, stride=cx * cy), :] for k in range(step)]
            high, low = split(jnp.concatenate(cols, axis=1))
            both = jnp.concatenate([high, low], axis=0)
            at = (x * groups + g) * wide
            hl[:, at : at + wide] = both
            total = total + lax.dot_general(both, both, NT, preferred_element_type=F32)
    ub[:, 0 : 2 * SP] = total
    full = ub[0:SP] + ub[SP:] + pltpu.roll(ub[0:SP], LANES - SP, 1)
    lane = lax.broadcasted_iota(jnp.int32, (8, LANES), 1)
    starts = range(0, species, 8)
    shifts = [sum(species - a for a in starts[:b]) - at for b, at in enumerate(starts)]
    packed = jnp.zeros((8, LANES), F32)
    for at, shift in zip(starts, shifts):
        rows = jnp.where((lane >= at) & (lane < species), full[at : at + 8], 0.0)
        packed = packed + (pltpu.roll(rows, shift, 1) if shift else rows)

    pl.semaphore_wait(barrier, len(peers))

    def start_sum(value, buf, n, me, target):
        buf[me] = value
        return [send(buf.at[me], buf.at[me], target(d)) for d in range(1, n)]

    def end_sum(copies, buf, n):
        for copy in copies:
            copy.wait()
        out = buf[0]
        for k in range(1, n):
            out = out + buf[k]
        return out

    packed = end_sum(start_sum(packed, b_sa, ns, sa, to_sa), b_sa, ns)
    packed = end_sum(start_sum(packed, b_p, nx * ny, gy, to_plane), b_p, nx * ny)
    copies = start_sum(packed, b_z, nz, gx, to_z)
    w = wb[...]
    w = orth(orth(w, ranks), ranks)
    packed = end_sum(copies, b_z, nz)

    scale = 1.0 / cfg["cells"]
    packed = packed * scale
    zb[...] = jnp.zeros(zb.shape, F32)
    for at, shift in zip(starts, shifts):
        rows = pltpu.roll(packed, LANES - shift, 1) if shift else packed
        zb[at : at + 8] = jnp.where((lane >= at) & (lane < species), rows, 0.0)
    upper = zb[...]
    row = lax.broadcasted_iota(jnp.int32, zb.shape, 0)
    column = lax.broadcasted_iota(jnp.int32, zb.shape, 1)
    gram = upper + jnp.where(column >= (row & ~7) + 8, upper, 0.0).T
    gram = gram + pltpu.roll(gram, GROUP, 1) + pltpu.roll(gram, 2 * GROUP, 1)

    def round_(i, w):
        w = jnp.dot(w, gram, precision=HIGH, preferred_element_type=F32)
        return orth(orth(w, ranks), ranks)

    w = lax.fori_loop(0, ITERS, round_, w)

    w = jnp.where(lax.broadcasted_iota(jnp.int32, w.shape, 1) < species, w, 0.0)
    whigh = w.astype(BF16).astype(F32)
    lhs = jnp.concatenate([whigh + pltpu.roll(whigh, SP, 1), w - whigh], axis=0).astype(BF16)
    lhs = lhs[:, 0 : 2 * SP]
    cflat = core.reshape(ranks * cx * YP, cz)

    def project(x):
        for g in range(groups):
            at = (x * groups + g) * wide
            out = jnp.dot(lhs, hl[:, at : at + wide], preferred_element_type=F32)
            out = out[0:ranks] + out[ranks:]
            for k in range(step):
                cflat[pl.ds(x * YP + g * step + k, ranks, stride=cx * YP), :] = (
                    out[:, k * cz : (k + 1) * cz]
                )

    hx = cx // 2
    firsts = {}
    for a in range(hx):
        project(a)
        firsts[a] = []
        for d in range(1, nx):
            there = lax.rem(mx + d, nx)
            firsts[a].append(send(core.at[:, there, a, 0:cy], mid0.at[a, :, mx, 0:cy], to_x(d)))
        x = hx + a
        project(x)
        firsts[x] = []
        for d in range(1, ny):
            there = lax.rem(my + d, ny)
            firsts[x].append(send(core.at[there, :, x, 0:cy], mid1.at[a, :, my, 0:cy], to_y(d)))
    for a in range(hx):
        mid0[a, :, mx] = core[:, mx, a]
        mid1[a, :, my] = core[my, :, hx + a]
    both_out[48:64] = w
    seconds = {}
    for a in range(hx):
        for copy in firsts[a]:
            copy.wait()
        seconds[a] = []
        for d in range(1, ny):
            there = lax.rem(my + d, ny)
            seconds[a].append(send(mid0.at[a, there, :, 0:cy], recv.at[a, my, :, 0:cy], to_y(d)))
        recv[a, my] = mid0[a, my]
        x = hx + a
        for copy in firsts[x]:
            copy.wait()
        seconds[x] = []
        for d in range(1, nx):
            there = lax.rem(mx + d, nx)
            seconds[x].append(send(mid1.at[a, there, :, 0:cy], recv.at[x, :, mx, 0:cy], to_x(d)))
        recv[x, :, mx] = mid1[a, mx]

    rows = ny * nx * YP
    columns = nz * YP
    depth = cx * cz
    lrows = ah.reshape(ny, nx * YP, depth), al.reshape(ny, nx * YP, depth)

    def arrive(a):
        for at, x in ((2 * a, a), (2 * a + 1, hx + a)):
            for copy in seconds[x]:
                copy.wait()
            high, low = split(recv[x].reshape(rows, cz))
            ah[:, :, :, at * cz : (at + 1) * cz] = high.reshape(nz, ns, YP, cz)
            al[:, :, :, at * cz : (at + 1) * cz] = low.reshape(nz, ns, YP, cz)

    def gram_rows(y, side, a):
        part = slice(2 * a * cz, 2 * (a + 1) * cz)
        lh, ll = lrows[0][y, :, part], lrows[1][y, :, part]
        rh = ah[:, side, :, part].reshape(columns, 2 * cz)
        rl = al[:, side, :, part].reshape(columns, 2 * cz)
        out = (
            lax.dot_general(lh, rh, NT, preferred_element_type=F32)
            + lax.dot_general(lh, rl, NT, preferred_element_type=F32)
            + lax.dot_general(ll, rh, NT, preferred_element_type=F32)
        )
        return out.reshape(nx, YP, columns)

    for a in range(hx - 1):
        arrive(a)
        for y in range(ny):
            for side, sums in ((1 - sa, gs), (sa, go)):
                out = gram_rows(y, side, a)
                sums[y] = out if a == 0 else sums[y] + out
    arrive(hx - 1)

    hy = YP // 2
    order = [lax.rem(my + t, ny) for t in range(1, ny)] + [my]
    swaps, first0, first1 = [], {}, {}

    def theirs(t):
        y = order[t]
        gs[y] = gs[y] + gram_rows(y, 1 - sa, hx - 1)
        swaps.append(send(gs.at[y], gr.at[y], to_sa(1)))

    def ours(t):
        y = order[t]
        mine = go[y] + gram_rows(y, sa, hx - 1)
        swaps[t].wait()
        go[y] = mine + gr[y]
        for d in range(1, nx):
            there = lax.rem(mx + d, nx)
            first0[t, d] = send(go.at[y, there, 0:hy, :], r1a.at[d - 1, y], to_x(d))
        if t < ny - 1:
            for d in list(range(1, nx)) + [0]:
                there = lax.rem(mx + d, nx)
                first1[t, d] = send(go.at[y, there, hy:YP, :], r1b.at[t, there], to_y(t + 1))

    theirs(0)
    for t in range(1, ny):
        theirs(t)
        ours(t - 1)
    ours(ny - 1)
    def sum0(t):
        y = order[t]
        out = go[y, mx, 0:hy, :]
        for d in range(1, nx):
            first0[t, d].wait()
            out = out + r1a[d - 1, y]
        return out

    def sum1(d):
        there = lax.rem(mx + d, nx)
        out = go[my, there, hy:YP, :]
        for t in range(ny - 1):
            first1[t, d].wait()
            out = out + r1b[t, there]
        return out

    second0, second1 = [], []
    for k in range(max(nx, ny) - 1):
        if k < ny - 1:
            t0[k] = sum0(k)
            second0.append(send(t0.at[k], r2a.at[k], to_y(k + 1)))
        if k < nx - 1:
            t1[k] = sum1(k + 1)
            second1.append(send(t1.at[k], r2b.at[k], to_x(k + 1)))
    out0, out1 = sum0(ny - 1), sum1(0)
    for k in range(ny - 1):
        second0[k].wait()
        out0 = out0 + r2a[k]
    for k in range(nx - 1):
        second1[k].wait()
        out1 = out1 + r2b[k]
    hb[0:hy, 0 : nz * YP] = out0
    hb[hy:YP, 0 : nz * YP] = out1

    lane = lax.broadcasted_iota(jnp.int32, (16, LANES), 1)
    for g in range(nz):
        tile = (g * YP) // LANES
        at = g * YP - tile * LANES
        parts = []
        for part in (hb[0:16], hb[16:32], hb[32:48]):
            piece = part[:, tile * LANES : (tile + 1) * LANES]
            if at:
                piece = pltpu.roll(piece, LANES - at, 1)
            if at + YP > LANES:
                other = part[:, (tile + 1) * LANES : (tile + 2) * LANES]
                piece = jnp.where(lane < LANES - at, piece, pltpu.roll(other, LANES - at, 1))
            parts.append(piece)
        moved = jnp.where(lane < 2 * cy, pltpu.roll(parts[1], cy, 1), pltpu.roll(parts[2], 2 * cy, 1))
        pack[g] = jnp.where(lane < cy, parts[0], moved)
    last = []
    for d in range(1, nz):
        last.append(send(pack.at[lax.rem(gx + d, nz)], r3.at[d - 1], to_z(d)))
    out = pack[gx]
    for copy in last:
        copy.wait()
    for d in range(1, nz):
        out = out + r3[d - 1]
    out = out * (1.0 / cfg["terms"])
    both_out[0:16] = out
    both_out[16:32] = pltpu.roll(out, LANES - cy, 1)
    both_out[32:48] = pltpu.roll(out, LANES - 2 * cy, 1)


def tail(species, cy, both, basis, block):
    basis[...] = both[48:64, 0:species]
    block[...] = both[0:cy, 0:cy]


def on_device(cfg, field, start):
    species, cx, cy, cz = field.shape
    ranks = start.shape[1]
    nx, ny, nz = cfg["nx"], cfg["ny"], cfg["nz"]
    cols = nz * YP
    colsp = -(-cols // LANES) * LANES
    hy = YP // 2
    hx = cx // 2
    cells = cx * cy * cz
    ring = nx + ny - 2
    copies = 1 + nx * ny - 1 + nz - 1 + 2 * hx * ring + ny + 2 * nx * ny - nx - ny + nx * (ny - 1) + ring + nz
    vmem = pltpu.VMEM
    scratch = [
        vmem((SP, cx * cy, cz), F32), vmem((2 * SP, cells), BF16), vmem((2 * SP, LANES), F32),
        vmem((LANES, LANES), F32), vmem((ranks, LANES), F32), vmem((2, 8, LANES), F32), vmem((nx * ny, 8, LANES), F32), vmem((nz, 8, LANES), F32),
        vmem((ny, nx, cx, YP, cz), F32), vmem((hx, ny, nx, YP, cz), F32),
        vmem((hx, nx, ny, YP, cz), F32), vmem((cx, ny, nx, YP, cz), F32),
        vmem((nz, 2, YP, cx * cz), BF16), vmem((nz, 2, YP, cx * cz), BF16),
        vmem((ny, nx, YP, cols), F32), vmem((ny, nx, YP, cols), F32), vmem((ny, nx, YP, cols), F32),
        vmem((nx - 1, ny, hy, cols), F32), vmem((ny - 1, nx, hy, cols), F32),
        vmem((ny - 1, hy, cols), F32), vmem((nx - 1, hy, cols), F32),
        vmem((ny - 1, hy, cols), F32), vmem((nx - 1, hy, cols), F32),
        vmem((YP, colsp), F32), vmem((nz, 16, LANES), F32), vmem((nz - 1, 16, LANES), F32),
        pltpu.SemaphoreType.DMA((cfg["cy"] // cfg["step"],)), pltpu.SemaphoreType.DMA((copies,)), pltpu.SemaphoreType.DMA((copies,)),
    ]
    both = pl.pallas_call(
        functools.partial(kernel, cfg),
        out_shape=jax.ShapeDtypeStruct((64, LANES), F32),
        in_specs=[pl.BlockSpec(memory_space=pl.ANY), pl.BlockSpec(memory_space=vmem)],
        out_specs=pl.BlockSpec(memory_space=vmem),
        scratch_shapes=scratch,
        compiler_params=pltpu.CompilerParams(
            collective_id=0, has_side_effects=True, vmem_limit_bytes=56 * 1024 * 1024
        ),
        name="tucker_step",
    )(field.transpose(0, 2, 1, 3).reshape(species, cx * cy, cz), start.T)
    basis, block = pl.pallas_call(
        functools.partial(tail, species, cy),
        out_shape=(
            jax.ShapeDtypeStruct((ranks, species), F32),
            jax.ShapeDtypeStruct((cy, cy), F32),
        ),
        in_specs=[pl.BlockSpec(memory_space=vmem)],
        out_specs=(pl.BlockSpec(memory_space=vmem), pl.BlockSpec(memory_space=vmem)),
        name="parts",
    )(both)
    return basis.T, block


def solution(mesh):
    nz, n_plane, ns = mesh.shape["gx"], mesh.shape["gy"], mesh.shape["sa"]
    nx = math.isqrt(n_plane)
    cfg = dict(nx=nx, ny=n_plane // nx, nz=nz)

    def run(field, start):
        species, cx, cy, cz = field.shape
        ranks = start.shape[1]
        total = cx * nz * cz * ns
        full = dict(cfg, cx=cx, cy=cy, step=14 if cy % 14 == 0 else cy, cells=total * cy * n_plane, terms=ranks * total)
        return on_device(full, field, start)

    return jax.shard_map(
        run, mesh=mesh, in_specs=(P(None, "gx", "gy", "sa"), P()),
        out_specs=(P(), P("gy", ("gx", "sa"))), check_vma=False,
    )
```

```python
import functools
import math

import jax
import jax.numpy as jnp
from jax import lax
from jax.experimental import pallas as pl
from jax.experimental.pallas import tpu as pltpu
from jax.sharding import PartitionSpec as P

ITERS = 4
F32 = jnp.float32
BF16 = jnp.bfloat16
HIGH = lax.Precision.HIGHEST
LANES = 128
SP = 48
YP = 48
GROUP = 40
NT = (((1,), (1,)), ((), ()))


def split(value):
    high = value.astype(BF16)
    return high, (value - high.astype(F32)).astype(BF16)


def far_first(n):
    return sorted(range(1, n), key=lambda d: -min(d, n - d))


def orth(w, ranks):
    products = (w[:, None, :] * w[None, :, :]).reshape(ranks * ranks, LANES)
    lane = lax.broadcasted_iota(jnp.int32, products.shape, 1)
    first = products.astype(BF16).astype(F32)
    rest = products - first
    second = rest.astype(BF16).astype(F32)
    pieces = jnp.where(lane < GROUP, first, jnp.where(lane < 2 * GROUP, second, rest - second))
    ones = jnp.ones((LANES, LANES), BF16)
    inner = jnp.dot(pieces.astype(BF16), ones, preferred_element_type=F32)
    lines = [inner[i * ranks : (i + 1) * ranks] for i in range(ranks)]
    row = lax.broadcasted_iota(jnp.int32, (ranks, LANES), 0)
    pivots = jnp.ones((ranks, LANES), F32)
    for j in range(ranks):
        line = lines[j]
        pivots = jnp.where(row == j, line, pivots)
        factor = line * (1.0 / line[j : j + 1])
        if j + 1 < ranks:
            below = jnp.where(row > j, factor, 0.0)
            w = w - below * w[j : j + 1]
            for i in range(j + 1, ranks):
                lines[i] = lines[i] - factor[i : i + 1] * line
    return w * lax.rsqrt(pivots)


def kernel(cfg, field, start, both_out, fv, hl, ub, zb, wb, b_sa, b_p, b_z,
           core, mid0, mid1, recv, ah, al, gs, go, gr, r1a, r1b, t0, t1, r2a, r2b, hb, pack, r3,
           load_sem, ssem, rsem):
    nx, ny, nz, ns = cfg["nx"], cfg["ny"], cfg["nz"], 2
    species, cz = field.shape[0], field.shape[2]
    cx, cy = cfg["cx"], cfg["cy"]
    ranks = start.shape[0]
    gx, gy, sa = lax.axis_index("gx"), lax.axis_index("gy"), lax.axis_index("sa")
    mx, my = lax.rem(gy, nx), gy // nx

    def to_sa(d):
        return {"sa": 1 - sa}

    def to_x(d):
        return {"gy": my * nx + lax.rem(mx + d, nx)}

    def to_y(d):
        return {"gy": lax.rem(my + d, ny) * nx + mx}

    def to_plane(d):
        return {"gy": lax.rem(my + d // nx, ny) * nx + lax.rem(mx + d % nx, nx)}

    def to_z(d):
        return {"gx": lax.rem(gx + d, nz)}

    used = [0]

    def send(src, dst, target):
        k = used[0]
        used[0] += 1
        copy = pltpu.make_async_remote_copy(
            src_ref=src, dst_ref=dst, send_sem=ssem.at[k], recv_sem=rsem.at[k],
            device_id=target, device_id_type=pl.DeviceIdType.MESH,
        )
        copy.start()
        return copy

    step = cfg["step"]
    groups = cy // step
    loads = []
    for g in range(groups):
        part = pl.ds(g * step * cx, step * cx)
        loads.append(pltpu.make_async_copy(field.at[:, part], fv.at[0:species, part], load_sem.at[g]))
        loads[g].start()
    barrier = pltpu.get_barrier_semaphore()
    peers = [to_sa(1)] + [to_plane(d) for d in range(1, nx * ny)]
    peers += [to_z(d) for d in range(1, nz)]
    for peer in peers:
        pl.semaphore_signal(barrier, inc=1, device_id=peer, device_id_type=pl.DeviceIdType.MESH)
    fv[species:SP] = jnp.zeros((SP - species, cx * cy, cz), F32)
    ub[...] = jnp.zeros(ub.shape, F32)
    wb[...] = jnp.zeros(wb.shape, F32)
    for c in range(3):
        wb[:, c * GROUP : c * GROUP + species] = start[...]

    flat = fv.reshape(SP * cx * cy, cz)
    wide = step * cz
    total = jnp.zeros((2 * SP, 2 * SP), F32)
    for g in range(groups):
        loads[g].wait()
        for x in range(cx):
            cols = [flat[pl.ds((g * step + k) * cx + x, SP, stride=cx * cy), :] for k in range(step)]
            high, low = split(jnp.concatenate(cols, axis=1))
            both = jnp.concatenate([high, low], axis=0)
            at = (x * groups + g) * wide
            hl[:, at : at + wide] = both
            total = total + lax.dot_general(both, both, NT, preferred_element_type=F32)
    ub[:, 0 : 2 * SP] = total
    full = ub[0:SP] + ub[SP:] + pltpu.roll(ub[0:SP], LANES - SP, 1)
    lane = lax.broadcasted_iota(jnp.int32, (8, LANES), 1)
    starts = range(0, species, 8)
    shifts = [sum(species - a for a in starts[:b]) - at for b, at in enumerate(starts)]
    packed = jnp.zeros((8, LANES), F32)
    for at, shift in zip(starts, shifts):
        rows = jnp.where((lane >= at) & (lane < species), full[at : at + 8], 0.0)
        packed = packed + (pltpu.roll(rows, shift, 1) if shift else rows)

    pl.semaphore_wait(barrier, len(peers))

    def start_sum(value, buf, offsets, me, target):
        buf[me] = value
        return [send(buf.at[me], buf.at[me], target(d)) for d in offsets]

    def end_sum(copies, buf, n):
        for copy in copies:
            copy.wait()
        out = buf[0]
        for k in range(1, n):
            out = out + buf[k]
        return out

    packed = end_sum(start_sum(packed, b_sa, [1], sa, to_sa), b_sa, ns)
    plane = sorted(range(1, nx * ny), key=lambda d: -(min(d // nx, ny - d // nx) + min(d % nx, nx - d % nx)))
    packed = end_sum(start_sum(packed, b_p, plane, gy, to_plane), b_p, nx * ny)
    copies = start_sum(packed, b_z, far_first(nz), gx, to_z)
    w = wb[...]
    w = orth(orth(w, ranks), ranks)
    packed = end_sum(copies, b_z, nz)

    scale = 1.0 / cfg["cells"]
    packed = packed * scale
    zb[...] = jnp.zeros(zb.shape, F32)
    for at, shift in zip(starts, shifts):
        rows = pltpu.roll(packed, LANES - shift, 1) if shift else packed
        zb[at : at + 8] = jnp.where((lane >= at) & (lane < species), rows, 0.0)
    upper = zb[...]
    row = lax.broadcasted_iota(jnp.int32, zb.shape, 0)
    column = lax.broadcasted_iota(jnp.int32, zb.shape, 1)
    gram = upper + jnp.where(column >= (row & ~7) + 8, upper, 0.0).T
    gram = gram + pltpu.roll(gram, GROUP, 1) + pltpu.roll(gram, 2 * GROUP, 1)

    def round_(i, w):
        w = jnp.dot(w, gram, precision=HIGH, preferred_element_type=F32)
        return orth(orth(w, ranks), ranks)

    w = lax.fori_loop(0, ITERS, round_, w)

    w = jnp.where(lax.broadcasted_iota(jnp.int32, w.shape, 1) < species, w, 0.0)
    whigh = w.astype(BF16).astype(F32)
    lhs = jnp.concatenate([whigh + pltpu.roll(whigh, SP, 1), w - whigh], axis=0).astype(BF16)
    lhs = lhs[:, 0 : 2 * SP]
    cflat = core.reshape(ranks * cx * YP, cz)

    def project(x):
        for g in range(groups):
            at = (x * groups + g) * wide
            out = jnp.dot(lhs, hl[:, at : at + wide], preferred_element_type=F32)
            out = out[0:ranks] + out[ranks:]
            for k in range(step):
                cflat[pl.ds(x * YP + g * step + k, ranks, stride=cx * YP), :] = (
                    out[:, k * cz : (k + 1) * cz]
                )

    hx = cx // 2
    firsts = {}
    for a in range(hx):
        project(a)
        firsts[a] = []
        for d in far_first(nx):
            there = lax.rem(mx + d, nx)
            firsts[a].append(send(core.at[:, there, a, 0:cy], mid0.at[a, :, mx, 0:cy], to_x(d)))
        x = hx + a
        project(x)
        firsts[x] = []
        for d in far_first(ny):
            there = lax.rem(my + d, ny)
            firsts[x].append(send(core.at[there, :, x, 0:cy], mid1.at[a, :, my, 0:cy], to_y(d)))
    for a in range(hx):
        mid0[a, :, mx] = core[:, mx, a]
        mid1[a, :, my] = core[my, :, hx + a]
    both_out[48:64] = w
    seconds = {}
    for a in range(hx):
        for copy in firsts[a]:
            copy.wait()
        seconds[a] = []
        for d in far_first(ny):
            there = lax.rem(my + d, ny)
            seconds[a].append(send(mid0.at[a, there, :, 0:cy], recv.at[a, my, :, 0:cy], to_y(d)))
        recv[a, my] = mid0[a, my]
        x = hx + a
        for copy in firsts[x]:
            copy.wait()
        seconds[x] = []
        for d in far_first(nx):
            there = lax.rem(mx + d, nx)
            seconds[x].append(send(mid1.at[a, there, :, 0:cy], recv.at[x, :, mx, 0:cy], to_x(d)))
        recv[x, :, mx] = mid1[a, mx]

    rows = ny * nx * YP
    columns = nz * YP
    depth = cx * cz
    lrows = ah.reshape(ny, nx * YP, depth), al.reshape(ny, nx * YP, depth)

    def arrive(a):
        for at, x in ((2 * a, a), (2 * a + 1, hx + a)):
            for copy in seconds[x]:
                copy.wait()
            high, low = split(recv[x].reshape(rows, cz))
            ah[:, :, :, at * cz : (at + 1) * cz] = high.reshape(nz, ns, YP, cz)
            al[:, :, :, at * cz : (at + 1) * cz] = low.reshape(nz, ns, YP, cz)

    def gram_rows(y, side, a):
        part = slice(2 * a * cz, 2 * (a + 1) * cz)
        lh, ll = lrows[0][y, :, part], lrows[1][y, :, part]
        rh = ah[:, side, :, part].reshape(columns, 2 * cz)
        rl = al[:, side, :, part].reshape(columns, 2 * cz)
        out = (
            lax.dot_general(lh, rh, NT, preferred_element_type=F32)
            + lax.dot_general(lh, rl, NT, preferred_element_type=F32)
            + lax.dot_general(ll, rh, NT, preferred_element_type=F32)
        )
        return out.reshape(nx, YP, columns)

    for a in range(hx - 1):
        arrive(a)
        for y in range(ny):
            for side, sums in ((1 - sa, gs), (sa, go)):
                out = gram_rows(y, side, a)
                sums[y] = out if a == 0 else sums[y] + out
    arrive(hx - 1)

    hy = YP // 2
    offs = far_first(ny)
    order = [lax.rem(my + d, ny) for d in offs] + [my]
    swaps, first0, first1 = [], {}, {}

    def theirs(t):
        y = order[t]
        gs[y] = gs[y] + gram_rows(y, 1 - sa, hx - 1)
        swaps.append(send(gs.at[y], gr.at[y], to_sa(1)))

    def ours(t):
        y = order[t]
        mine = go[y] + gram_rows(y, sa, hx - 1)
        swaps[t].wait()
        go[y] = mine + gr[y]
        for d in far_first(nx):
            there = lax.rem(mx + d, nx)
            first0[t, d] = send(go.at[y, there, 0:hy, :], r1a.at[d - 1, y], to_x(d))
        if t < ny - 1:
            for d in far_first(nx) + [0]:
                there = lax.rem(mx + d, nx)
                first1[t, d] = send(go.at[y, there, hy:YP, :], r1b.at[t, there], to_y(offs[t]))

    theirs(0)
    for t in range(1, ny):
        theirs(t)
        ours(t - 1)
    ours(ny - 1)
    def sum0(t):
        y = order[t]
        out = go[y, mx, 0:hy, :]
        for d in range(1, nx):
            first0[t, d].wait()
            out = out + r1a[d - 1, y]
        return out

    def sum1(d):
        there = lax.rem(mx + d, nx)
        out = go[my, there, hy:YP, :]
        for t in range(ny - 1):
            first1[t, d].wait()
            out = out + r1b[t, there]
        return out

    second0, second1 = [], []
    for k in range(ny - 1):
        t0[k] = sum0(k)
        second0.append(send(t0.at[k], r2a.at[k], to_y(offs[k])))
    for k, d in enumerate(far_first(nx)):
        t1[k] = sum1(d)
        second1.append(send(t1.at[k], r2b.at[k], to_x(d)))
    out0, out1 = sum0(ny - 1), sum1(0)
    for k in range(ny - 1):
        second0[k].wait()
        out0 = out0 + r2a[k]
    for k in range(nx - 1):
        second1[k].wait()
        out1 = out1 + r2b[k]
    hb[0:hy, 0 : nz * YP] = out0
    hb[hy:YP, 0 : nz * YP] = out1

    lane = lax.broadcasted_iota(jnp.int32, (16, LANES), 1)
    for g in range(nz):
        tile = (g * YP) // LANES
        at = g * YP - tile * LANES
        parts = []
        for part in (hb[0:16], hb[16:32], hb[32:48]):
            piece = part[:, tile * LANES : (tile + 1) * LANES]
            if at:
                piece = pltpu.roll(piece, LANES - at, 1)
            if at + YP > LANES:
                other = part[:, (tile + 1) * LANES : (tile + 2) * LANES]
                piece = jnp.where(lane < LANES - at, piece, pltpu.roll(other, LANES - at, 1))
            parts.append(piece)
        moved = jnp.where(lane < 2 * cy, pltpu.roll(parts[1], cy, 1), pltpu.roll(parts[2], 2 * cy, 1))
        pack[g] = jnp.where(lane < cy, parts[0], moved)
    last = []
    for d in far_first(nz):
        last.append(send(pack.at[lax.rem(gx + d, nz)], r3.at[d - 1], to_z(d)))
    out = pack[gx]
    for copy in last:
        copy.wait()
    for d in range(1, nz):
        out = out + r3[d - 1]
    out = out * (1.0 / cfg["terms"])
    both_out[0:16] = out
    both_out[16:32] = pltpu.roll(out, LANES - cy, 1)
    both_out[32:48] = pltpu.roll(out, LANES - 2 * cy, 1)


def tail(species, cy, both, basis, block):
    basis[...] = both[48:64, 0:species]
    block[...] = both[0:cy, 0:cy]


def on_device(cfg, field, start):
    species, cx, cy, cz = field.shape
    ranks = start.shape[1]
    nx, ny, nz = cfg["nx"], cfg["ny"], cfg["nz"]
    cols = nz * YP
    colsp = -(-cols // LANES) * LANES
    hy = YP // 2
    hx = cx // 2
    cells = cx * cy * cz
    ring = nx + ny - 2
    copies = 1 + nx * ny - 1 + nz - 1 + 2 * hx * ring + ny + 2 * nx * ny - nx - ny + nx * (ny - 1) + ring + nz
    vmem = pltpu.VMEM
    scratch = [
        vmem((SP, cx * cy, cz), F32), vmem((2 * SP, cells), BF16), vmem((2 * SP, LANES), F32),
        vmem((LANES, LANES), F32), vmem((ranks, LANES), F32), vmem((2, 8, LANES), F32), vmem((nx * ny, 8, LANES), F32), vmem((nz, 8, LANES), F32),
        vmem((ny, nx, cx, YP, cz), F32), vmem((hx, ny, nx, YP, cz), F32),
        vmem((hx, nx, ny, YP, cz), F32), vmem((cx, ny, nx, YP, cz), F32),
        vmem((nz, 2, YP, cx * cz), BF16), vmem((nz, 2, YP, cx * cz), BF16),
        vmem((ny, nx, YP, cols), F32), vmem((ny, nx, YP, cols), F32), vmem((ny, nx, YP, cols), F32),
        vmem((nx - 1, ny, hy, cols), F32), vmem((ny - 1, nx, hy, cols), F32),
        vmem((ny - 1, hy, cols), F32), vmem((nx - 1, hy, cols), F32),
        vmem((ny - 1, hy, cols), F32), vmem((nx - 1, hy, cols), F32),
        vmem((YP, colsp), F32), vmem((nz, 16, LANES), F32), vmem((nz - 1, 16, LANES), F32),
        pltpu.SemaphoreType.DMA((cfg["cy"] // cfg["step"],)), pltpu.SemaphoreType.DMA((copies,)), pltpu.SemaphoreType.DMA((copies,)),
    ]
    both = pl.pallas_call(
        functools.partial(kernel, cfg),
        out_shape=jax.ShapeDtypeStruct((64, LANES), F32),
        in_specs=[pl.BlockSpec(memory_space=pl.ANY), pl.BlockSpec(memory_space=vmem)],
        out_specs=pl.BlockSpec(memory_space=vmem),
        scratch_shapes=scratch,
        compiler_params=pltpu.CompilerParams(
            collective_id=0, has_side_effects=True, vmem_limit_bytes=56 * 1024 * 1024
        ),
        name="tucker_step",
    )(field.transpose(0, 2, 1, 3).reshape(species, cx * cy, cz), start.T)
    basis, block = pl.pallas_call(
        functools.partial(tail, species, cy),
        out_shape=(
            jax.ShapeDtypeStruct((ranks, species), F32),
            jax.ShapeDtypeStruct((cy, cy), F32),
        ),
        in_specs=[pl.BlockSpec(memory_space=vmem)],
        out_specs=(pl.BlockSpec(memory_space=vmem), pl.BlockSpec(memory_space=vmem)),
        name="parts",
    )(both)
    return basis.T, block


def solution(mesh):
    nz, n_plane, ns = mesh.shape["gx"], mesh.shape["gy"], mesh.shape["sa"]
    nx = math.isqrt(n_plane)
    cfg = dict(nx=nx, ny=n_plane // nx, nz=nz)

    def run(field, start):
        species, cx, cy, cz = field.shape
        ranks = start.shape[1]
        total = cx * nz * cz * ns
        full = dict(cfg, cx=cx, cy=cy, step=14 if cy % 14 == 0 else cy, cells=total * cy * n_plane, terms=ranks * total)
        return on_device(full, field, start)

    return jax.shard_map(
        run, mesh=mesh, in_specs=(P(None, "gx", "gy", "sa"), P()),
        out_specs=(P(), P("gy", ("gx", "sa"))), check_vma=False,
    )
```

```python
import functools
import math

import jax
import jax.numpy as jnp
from jax import lax
from jax.experimental import pallas as pl
from jax.experimental.pallas import tpu as pltpu
from jax.sharding import PartitionSpec as P

ITERS = 4
F32 = jnp.float32
BF16 = jnp.bfloat16
LANES = 128
SP = 48
YP = 48
GROUP = 40
NT = (((1,), (1,)), ((), ()))


def split(value):
    high = value.astype(BF16)
    return high, (value - high.astype(F32)).astype(BF16)


def pieces(value):
    lane = lax.broadcasted_iota(jnp.int32, value.shape, 1)
    first = value.astype(BF16).astype(F32)
    rest = value - first
    second = rest.astype(BF16).astype(F32)
    return jnp.where(lane < GROUP, first, jnp.where(lane < 2 * GROUP, second, rest - second)).astype(BF16)


def far_first(n):
    return sorted(range(1, n), key=lambda d: -min(d, n - d))


def orth(w, ranks):
    products = (w[:, None, :] * w[None, :, :]).reshape(ranks * ranks, LANES)
    ones = jnp.ones((LANES, LANES), BF16)
    inner = jnp.dot(pieces(products), ones, preferred_element_type=F32)
    lines = [inner[i * ranks : (i + 1) * ranks] for i in range(ranks)]
    row = lax.broadcasted_iota(jnp.int32, (ranks, LANES), 0)
    pivots = jnp.ones((ranks, LANES), F32)
    for j in range(ranks):
        line = lines[j]
        pivots = jnp.where(row == j, line, pivots)
        factor = line * (1.0 / line[j : j + 1])
        if j + 1 < ranks:
            below = jnp.where(row > j, factor, 0.0)
            w = w - below * w[j : j + 1]
            for i in range(j + 1, ranks):
                lines[i] = lines[i] - factor[i : i + 1] * line
    return w * lax.rsqrt(pivots)


def kernel(cfg, field, start, both_out, fv, hl, ub, zb, wb, b_sa, b_p, b_z,
           core, mid0, mid1, recv, ah, al, gs, go, gr, r1a, r1b, t0, t1, r2a, r2b, hb, pack, r3,
           load_sem, ssem, rsem):
    nx, ny, nz, ns = cfg["nx"], cfg["ny"], cfg["nz"], 2
    species, cz = field.shape[0], field.shape[2]
    cx, cy = cfg["cx"], cfg["cy"]
    ranks = start.shape[0]
    gx, gy, sa = lax.axis_index("gx"), lax.axis_index("gy"), lax.axis_index("sa")
    mx, my = lax.rem(gy, nx), gy // nx

    def to_sa(d):
        return {"sa": 1 - sa}

    def to_x(d):
        return {"gy": my * nx + lax.rem(mx + d, nx)}

    def to_y(d):
        return {"gy": lax.rem(my + d, ny) * nx + mx}

    def to_plane(d):
        return {"gy": lax.rem(my + d // nx, ny) * nx + lax.rem(mx + d % nx, nx)}

    def to_z(d):
        return {"gx": lax.rem(gx + d, nz)}

    used = [0]

    def send(src, dst, target):
        k = used[0]
        used[0] += 1
        copy = pltpu.make_async_remote_copy(
            src_ref=src, dst_ref=dst, send_sem=ssem.at[k], recv_sem=rsem.at[k],
            device_id=target, device_id_type=pl.DeviceIdType.MESH,
        )
        copy.start()
        return copy

    step = cfg["step"]
    groups = cy // step
    loads = []
    for g in range(groups):
        part = pl.ds(g * step * cx, step * cx)
        loads.append(pltpu.make_async_copy(field.at[:, part], fv.at[0:species, part], load_sem.at[g]))
        loads[g].start()
    barrier = pltpu.get_barrier_semaphore()
    peers = [to_sa(1)] + [to_plane(d) for d in range(1, nx * ny)]
    peers += [to_z(d) for d in range(1, nz)]
    for peer in peers:
        pl.semaphore_signal(barrier, inc=1, device_id=peer, device_id_type=pl.DeviceIdType.MESH)
    fv[species:SP] = jnp.zeros((SP - species, cx * cy, cz), F32)
    ub[...] = jnp.zeros(ub.shape, F32)
    wb[...] = jnp.zeros(wb.shape, F32)
    for c in range(3):
        wb[:, c * GROUP : c * GROUP + species] = start[...]

    flat = fv.reshape(SP * cx * cy, cz)
    wide = step * cz
    total = jnp.zeros((2 * SP, 2 * SP), F32)
    for g in range(groups):
        loads[g].wait()
        for x in range(cx):
            cols = [flat[pl.ds((g * step + k) * cx + x, SP, stride=cx * cy), :] for k in range(step)]
            high, low = split(jnp.concatenate(cols, axis=1))
            both = jnp.concatenate([high, low], axis=0)
            at = (x * groups + g) * wide
            hl[:, at : at + wide] = both
            total = total + lax.dot_general(both, both, NT, preferred_element_type=F32)
    ub[:, 0 : 2 * SP] = total
    full = ub[0:SP] + ub[SP:] + pltpu.roll(ub[0:SP], LANES - SP, 1)
    lane = lax.broadcasted_iota(jnp.int32, (8, LANES), 1)
    starts = range(0, species, 8)
    shifts = [sum(species - a for a in starts[:b]) - at for b, at in enumerate(starts)]
    packed = jnp.zeros((8, LANES), F32)
    for at, shift in zip(starts, shifts):
        rows = jnp.where((lane >= at) & (lane < species), full[at : at + 8], 0.0)
        packed = packed + (pltpu.roll(rows, shift, 1) if shift else rows)

    pl.semaphore_wait(barrier, len(peers))

    def start_sum(value, buf, offsets, me, target):
        buf[me] = value
        return [send(buf.at[me], buf.at[me], target(d)) for d in offsets]

    def end_sum(copies, buf, n):
        for copy in copies:
            copy.wait()
        out = buf[0]
        for k in range(1, n):
            out = out + buf[k]
        return out

    packed = end_sum(start_sum(packed, b_sa, [1], sa, to_sa), b_sa, ns)
    plane = sorted(range(1, nx * ny), key=lambda d: -(min(d // nx, ny - d // nx) + min(d % nx, nx - d % nx)))
    packed = end_sum(start_sum(packed, b_p, plane, gy, to_plane), b_p, nx * ny)
    copies = start_sum(packed, b_z, far_first(nz), gx, to_z)
    w = wb[...]
    w = orth(orth(w, ranks), ranks)
    packed = end_sum(copies, b_z, nz)

    scale = 1.0 / cfg["cells"]
    packed = packed * scale
    zb[...] = jnp.zeros(zb.shape, F32)
    for at, shift in zip(starts, shifts):
        rows = pltpu.roll(packed, LANES - shift, 1) if shift else packed
        zb[at : at + 8] = jnp.where((lane >= at) & (lane < species), rows, 0.0)
    upper = zb[...]
    row = lax.broadcasted_iota(jnp.int32, zb.shape, 0)
    column = lax.broadcasted_iota(jnp.int32, zb.shape, 1)
    gram = upper + jnp.where(column >= (row & ~7) + 8, upper, 0.0).T
    gram = gram + pltpu.roll(gram, GROUP, 1) + pltpu.roll(gram, 2 * GROUP, 1)

    gram = gram + pltpu.roll(gram, GROUP, 0) + pltpu.roll(gram, 2 * GROUP, 0)
    first, rest = split(gram)
    second, third = split(gram - first.astype(F32))
    grams = jnp.concatenate([first, second, third], axis=1)

    def round_(i, w):
        out = jnp.dot(pieces(w), grams, preferred_element_type=F32)
        w = out[:, 0:LANES] + out[:, LANES : 2 * LANES] + out[:, 2 * LANES :]
        return orth(orth(w, ranks), ranks)

    w = lax.fori_loop(0, ITERS, round_, w)

    w = jnp.where(lax.broadcasted_iota(jnp.int32, w.shape, 1) < species, w, 0.0)
    whigh = w.astype(BF16).astype(F32)
    lhs = jnp.concatenate([whigh + pltpu.roll(whigh, SP, 1), w - whigh], axis=0).astype(BF16)
    lhs = lhs[:, 0 : 2 * SP]
    cflat = core.reshape(ranks * cx * YP, cz)

    def project(x):
        for g in range(groups):
            at = (x * groups + g) * wide
            out = jnp.dot(lhs, hl[:, at : at + wide], preferred_element_type=F32)
            out = out[0:ranks] + out[ranks:]
            for k in range(step):
                cflat[pl.ds(x * YP + g * step + k, ranks, stride=cx * YP), :] = (
                    out[:, k * cz : (k + 1) * cz]
                )

    hx = cx // 2
    firsts = {}
    for a in range(hx):
        project(a)
        firsts[a] = []
        for d in far_first(nx):
            there = lax.rem(mx + d, nx)
            firsts[a].append(send(core.at[:, there, a, 0:cy], mid0.at[a, :, mx, 0:cy], to_x(d)))
        x = hx + a
        project(x)
        firsts[x] = []
        for d in far_first(ny):
            there = lax.rem(my + d, ny)
            firsts[x].append(send(core.at[there, :, x, 0:cy], mid1.at[a, :, my, 0:cy], to_y(d)))
    for a in range(hx):
        mid0[a, :, mx] = core[:, mx, a]
        mid1[a, :, my] = core[my, :, hx + a]
    both_out[48:64] = w
    seconds = {}
    for a in range(hx):
        for copy in firsts[a]:
            copy.wait()
        seconds[a] = []
        for d in far_first(ny):
            there = lax.rem(my + d, ny)
            seconds[a].append(send(mid0.at[a, there, :, 0:cy], recv.at[a, my, :, 0:cy], to_y(d)))
        recv[a, my] = mid0[a, my]
        x = hx + a
        for copy in firsts[x]:
            copy.wait()
        seconds[x] = []
        for d in far_first(nx):
            there = lax.rem(mx + d, nx)
            seconds[x].append(send(mid1.at[a, there, :, 0:cy], recv.at[x, :, mx, 0:cy], to_x(d)))
        recv[x, :, mx] = mid1[a, mx]

    rows = ny * nx * YP
    columns = nz * YP
    depth = cx * cz
    lrows = ah.reshape(ny, nx * YP, depth), al.reshape(ny, nx * YP, depth)

    def arrive(a):
        for at, x in ((2 * a, a), (2 * a + 1, hx + a)):
            for copy in seconds[x]:
                copy.wait()
            high, low = split(recv[x].reshape(rows, cz))
            ah[:, :, :, at * cz : (at + 1) * cz] = high.reshape(nz, ns, YP, cz)
            al[:, :, :, at * cz : (at + 1) * cz] = low.reshape(nz, ns, YP, cz)

    def gram_rows(y, side, a):
        part = slice(2 * a * cz, 2 * (a + 1) * cz)
        lh, ll = lrows[0][y, :, part], lrows[1][y, :, part]
        rh = ah[:, side, :, part].reshape(columns, 2 * cz)
        rl = al[:, side, :, part].reshape(columns, 2 * cz)
        out = (
            lax.dot_general(lh, rh, NT, preferred_element_type=F32)
            + lax.dot_general(lh, rl, NT, preferred_element_type=F32)
            + lax.dot_general(ll, rh, NT, preferred_element_type=F32)
        )
        return out.reshape(nx, YP, columns)

    for a in range(hx - 1):
        arrive(a)
        for y in range(ny):
            for side, sums in ((1 - sa, gs), (sa, go)):
                out = gram_rows(y, side, a)
                sums[y] = out if a == 0 else sums[y] + out
    arrive(hx - 1)

    hy = YP // 2
    offs = far_first(ny)
    order = [lax.rem(my + d, ny) for d in offs] + [my]
    swaps, first0, first1 = [], {}, {}

    def theirs(t):
        y = order[t]
        gs[y] = gs[y] + gram_rows(y, 1 - sa, hx - 1)
        swaps.append(send(gs.at[y], gr.at[y], to_sa(1)))

    def ours(t):
        y = order[t]
        mine = go[y] + gram_rows(y, sa, hx - 1)
        swaps[t].wait()
        go[y] = mine + gr[y]
        for d in far_first(nx):
            there = lax.rem(mx + d, nx)
            first0[t, d] = send(go.at[y, there, 0:hy, :], r1a.at[d - 1, y], to_x(d))
        if t < ny - 1:
            for d in far_first(nx) + [0]:
                there = lax.rem(mx + d, nx)
                first1[t, d] = send(go.at[y, there, hy:YP, :], r1b.at[t, there], to_y(offs[t]))

    theirs(0)
    for t in range(1, ny):
        theirs(t)
        ours(t - 1)
    ours(ny - 1)
    def sum0(t):
        y = order[t]
        out = go[y, mx, 0:hy, :]
        for d in range(1, nx):
            first0[t, d].wait()
            out = out + r1a[d - 1, y]
        return out

    def sum1(d):
        there = lax.rem(mx + d, nx)
        out = go[my, there, hy:YP, :]
        for t in range(ny - 1):
            first1[t, d].wait()
            out = out + r1b[t, there]
        return out

    second0, second1 = [], []
    for k in range(ny - 1):
        t0[k] = sum0(k)
        second0.append(send(t0.at[k], r2a.at[k], to_y(offs[k])))
    for k, d in enumerate(far_first(nx)):
        t1[k] = sum1(d)
        second1.append(send(t1.at[k], r2b.at[k], to_x(d)))
    out0, out1 = sum0(ny - 1), sum1(0)
    for k in range(ny - 1):
        second0[k].wait()
        out0 = out0 + r2a[k]
    for k in range(nx - 1):
        second1[k].wait()
        out1 = out1 + r2b[k]
    hb[0:hy, 0 : nz * YP] = out0
    hb[hy:YP, 0 : nz * YP] = out1

    lane = lax.broadcasted_iota(jnp.int32, (16, LANES), 1)
    for g in range(nz):
        tile = (g * YP) // LANES
        at = g * YP - tile * LANES
        parts = []
        for part in (hb[0:16], hb[16:32], hb[32:48]):
            piece = part[:, tile * LANES : (tile + 1) * LANES]
            if at:
                piece = pltpu.roll(piece, LANES - at, 1)
            if at + YP > LANES:
                other = part[:, (tile + 1) * LANES : (tile + 2) * LANES]
                piece = jnp.where(lane < LANES - at, piece, pltpu.roll(other, LANES - at, 1))
            parts.append(piece)
        moved = jnp.where(lane < 2 * cy, pltpu.roll(parts[1], cy, 1), pltpu.roll(parts[2], 2 * cy, 1))
        pack[g] = jnp.where(lane < cy, parts[0], moved)
    last = []
    for d in far_first(nz):
        last.append(send(pack.at[lax.rem(gx + d, nz)], r3.at[d - 1], to_z(d)))
    out = pack[gx]
    for copy in last:
        copy.wait()
    for d in range(1, nz):
        out = out + r3[d - 1]
    out = out * (1.0 / cfg["terms"])
    both_out[0:16] = out
    both_out[16:32] = pltpu.roll(out, LANES - cy, 1)
    both_out[32:48] = pltpu.roll(out, LANES - 2 * cy, 1)


def tail(species, cy, both, basis, block):
    basis[...] = both[48:64, 0:species]
    block[...] = both[0:cy, 0:cy]


def on_device(cfg, field, start):
    species, cx, cy, cz = field.shape
    ranks = start.shape[1]
    nx, ny, nz = cfg["nx"], cfg["ny"], cfg["nz"]
    cols = nz * YP
    colsp = -(-cols // LANES) * LANES
    hy = YP // 2
    hx = cx // 2
    cells = cx * cy * cz
    ring = nx + ny - 2
    copies = 1 + nx * ny - 1 + nz - 1 + 2 * hx * ring + ny + 2 * nx * ny - nx - ny + nx * (ny - 1) + ring + nz
    vmem = pltpu.VMEM
    scratch = [
        vmem((SP, cx * cy, cz), F32), vmem((2 * SP, cells), BF16), vmem((2 * SP, LANES), F32),
        vmem((LANES, LANES), F32), vmem((ranks, LANES), F32), vmem((2, 8, LANES), F32), vmem((nx * ny, 8, LANES), F32), vmem((nz, 8, LANES), F32),
        vmem((ny, nx, cx, YP, cz), F32), vmem((hx, ny, nx, YP, cz), F32),
        vmem((hx, nx, ny, YP, cz), F32), vmem((cx, ny, nx, YP, cz), F32),
        vmem((nz, 2, YP, cx * cz), BF16), vmem((nz, 2, YP, cx * cz), BF16),
        vmem((ny, nx, YP, cols), F32), vmem((ny, nx, YP, cols), F32), vmem((ny, nx, YP, cols), F32),
        vmem((nx - 1, ny, hy, cols), F32), vmem((ny - 1, nx, hy, cols), F32),
        vmem((ny - 1, hy, cols), F32), vmem((nx - 1, hy, cols), F32),
        vmem((ny - 1, hy, cols), F32), vmem((nx - 1, hy, cols), F32),
        vmem((YP, colsp), F32), vmem((nz, 16, LANES), F32), vmem((nz - 1, 16, LANES), F32),
        pltpu.SemaphoreType.DMA((cfg["cy"] // cfg["step"],)), pltpu.SemaphoreType.DMA((copies,)), pltpu.SemaphoreType.DMA((copies,)),
    ]
    both = pl.pallas_call(
        functools.partial(kernel, cfg),
        out_shape=jax.ShapeDtypeStruct((64, LANES), F32),
        in_specs=[pl.BlockSpec(memory_space=pl.ANY), pl.BlockSpec(memory_space=vmem)],
        out_specs=pl.BlockSpec(memory_space=vmem),
        scratch_shapes=scratch,
        compiler_params=pltpu.CompilerParams(
            collective_id=0, has_side_effects=True, vmem_limit_bytes=56 * 1024 * 1024
        ),
        name="tucker_step",
    )(field.transpose(0, 2, 1, 3).reshape(species, cx * cy, cz), start.T)
    basis, block = pl.pallas_call(
        functools.partial(tail, species, cy),
        out_shape=(
            jax.ShapeDtypeStruct((ranks, species), F32),
            jax.ShapeDtypeStruct((cy, cy), F32),
        ),
        in_specs=[pl.BlockSpec(memory_space=vmem)],
        out_specs=(pl.BlockSpec(memory_space=vmem), pl.BlockSpec(memory_space=vmem)),
        name="parts",
    )(both)
    return basis.T, block


def solution(mesh):
    nz, n_plane, ns = mesh.shape["gx"], mesh.shape["gy"], mesh.shape["sa"]
    nx = math.isqrt(n_plane)
    cfg = dict(nx=nx, ny=n_plane // nx, nz=nz)

    def run(field, start):
        species, cx, cy, cz = field.shape
        ranks = start.shape[1]
        total = cx * nz * cz * ns
        full = dict(cfg, cx=cx, cy=cy, step=14 if cy % 14 == 0 else cy, cells=total * cy * n_plane, terms=ranks * total)
        return on_device(full, field, start)

    return jax.shard_map(
        run, mesh=mesh, in_specs=(P(None, "gx", "gy", "sa"), P()),
        out_specs=(P(), P("gy", ("gx", "sa"))), check_vma=False,
    )
```
